32 devices in a mesh: grp: 2 (over y), row: 4 (over z), mic: 2 (over x), orient: 2 (over core).
Axes of the slice: x: 2, y: 2, z: 4, core: 2. Of those that a mesh axis runs over, the one named last changes fastest.
Arguments:
- spectra: bfloat16 [8, 2, 2048, 2048], P(('grp', 'mic'), None, 'row'), parts along dimension 0, may hold values from -6 to 6
- bank: bfloat16 [8, 384, 384], replicated, as said below
- orient_index: int32 [16], P('grp'), parts along dimension 0, may hold values from 0 to 7, as said below
Outputs:
- peak_map: float32 [8, 4, 512, 128], P(('grp', 'mic'), 'row'), parts along dimension 0
- power_map: float32 [8, 4, 512, 128], P(('grp', 'mic'), 'row'), parts along dimension 0
The draws below stay inside these ranges and needn't reach their ends.
There are 2 independent parts, one for each index of `grp`. The reference program is written for one: setup_inputs(seed, part) draws one part's arguments, and reference() takes and returns one part's arrays. A program takes and returns all parts, laid end to end along the dimension named above; an argument that names none is the same for every part. Nothing has to cross between parts.
Inputs may be any that keep to these rules, and one draw needn't show every extreme that they name: `bank`: projection images of the table. `orient_index`: each entry names one projection of the table; entries may repeat.
All inputs are finite; a program needn't handle non-finite values.
Results may differ from the reference program's by a relative error of at most 0.0051.
Values may be sent and summed in bfloat16 or wider, within the bound.
A program may use at most 128 MiB of HBM per device.

```python
import math
import jax
import jax.numpy as jnp
import numpy as np
from jax import lax

NFFT = 2048
TSIZE = 384
WCOLS = 128
WIN = 8
BANK = 8
MICS = 4
RBANDS = 4
YB = 512


def draw_bank(key, part):
    key_rows = jax.random.fold_in(key, 101)
    key_cols = jax.random.fold_in(key, 202)
    key_noise = jax.random.fold_in(key, 303)
    key_shift = jax.random.fold_in(key, 404)
    row_scale = jnp.exp(jax.random.uniform(key_rows, (BANK, TSIZE, 1), jnp.float32) * math.log(10.0))
    col_scale = jnp.exp(jax.random.uniform(key_cols, (BANK, 1, TSIZE), jnp.float32) * math.log(10.0))
    noise = jax.random.normal(key_noise, (BANK, TSIZE, TSIZE), jnp.float32)
    offset = jax.random.normal(key_shift, (BANK, 1, 1), jnp.float32)
    values = noise * row_scale * col_scale + 3.0 * offset
    return values.astype(jnp.bfloat16)


def draw_orient_index(key, part):
    key_values = jax.random.fold_in(key, 505)
    key_order = jax.random.fold_in(key, 606)
    values = jax.random.randint(key_values, (WIN,), 0, BANK, dtype=jnp.int32)
    order = jax.random.permutation(key_order, WIN)
    positions = jnp.arange(WIN, dtype=jnp.int32)
    values = jnp.where(positions == order[0], BANK - 1, values)
    values = jnp.where(positions == order[1], 0, values)
    return values.astype(jnp.int32)


def block_levels(own_key, shape, pieces, low, top_value):
    level = 1.0
    for dim, shards_of in pieces:
        heights = jax.random.uniform(jax.random.fold_in(jax.random.fold_in(own_key, 6), dim), (shards_of,), jnp.float32, low / len(pieces), top_value / len(pieces))
        level = level * jnp.repeat(jnp.exp(heights), shape[dim] // shards_of).reshape((-1,) + (1,) * (len(shape) - 1 - dim))
    return level


def bell_draw(key, shape, scale, reach, cuts=(), kind=jnp.bfloat16):
    values = jax.random.normal(key, shape, jnp.float32) * scale
    if len(cuts) > 0:
        values = block_levels(key, shape, cuts, -0.22, 0.18) * values
    return jnp.clip(values, min=-reach, max=reach).astype(kind)


def setup_inputs(seed: int = 0, part: int = 0) -> dict:
    keys = jax.random.split(jax.random.key(seed), 4)
    part_keys = jax.random.split(jax.random.fold_in(keys[3], part), 4)
    return {
        "spectra": bell_draw(part_keys[0], (MICS, 2, NFFT, NFFT), 1.0, 6.0, ((0, 2), (2, 4))),
        "bank": draw_bank(jax.random.fold_in(keys[3], 71), part),
        "orient_index": draw_orient_index(jax.random.fold_in(jax.random.fold_in(keys[3], part), 71), part),
    }


two_pi = 2.0 * math.pi

def phase_table(row_start, row_count, col_start, col_count, period):
    row_ids = row_start + jnp.arange(row_count, dtype=jnp.int32)
    col_ids = col_start + jnp.arange(col_count, dtype=jnp.int32)
    wrapped = row_ids[:, None] * col_ids[None, :] % period
    angles = wrapped.astype(jnp.float32) * (two_pi / period)
    return (jnp.cos(angles), jnp.sin(angles))

def normalize(picture):
    values = picture.astype(jnp.float32)
    centred = values - jnp.mean(values)
    factor = lax.rsqrt(jnp.mean(centred * centred) + 1e-06)
    return (centred * factor).astype(jnp.bfloat16)

def reverse_bits(number, digits):
    result = number * 0
    for digit in range(digits):
        result = result + number // (1 << digit) % 2 * (1 << digits - 1 - digit)
    return result

def reference(spectra, bank, orient_index):
    sections = RBANDS.bit_length() - 1
    templates = jax.vmap(normalize)(bank[orient_index])
    cos_y, sin_y = phase_table(0, NFFT, 0, TSIZE, NFFT)
    cos_x, sin_x = phase_table(0, TSIZE, 0, NFFT, NFFT)
    cos_e, sin_e = phase_table(0, NFFT, 0, WCOLS, NFFT)
    cos_y = cos_y.astype(jnp.bfloat16)
    neg_sin_y = -sin_y.astype(jnp.bfloat16)
    cos_x = cos_x.astype(jnp.bfloat16)
    sin_x = sin_x.astype(jnp.bfloat16)
    cos_e = cos_e.astype(jnp.bfloat16)
    sin_e = sin_e.astype(jnp.bfloat16)
    cos_c, sin_c = phase_table(0, NFFT, 0, NFFT, NFFT)
    factor = 1.0 / (NFFT * TSIZE)

    def one_orientation(template):
        pass_re = jnp.dot(cos_y, template, preferred_element_type=jnp.float32).astype(jnp.bfloat16)
        pass_im = jnp.dot(neg_sin_y, template, preferred_element_type=jnp.float32).astype(jnp.bfloat16)
        spec_re = (jnp.dot(pass_re, cos_x, preferred_element_type=jnp.float32) + jnp.dot(pass_im, sin_x, preferred_element_type=jnp.float32)).astype(jnp.bfloat16)
        spec_im = (jnp.dot(pass_im, cos_x, preferred_element_type=jnp.float32) - jnp.dot(pass_re, sin_x, preferred_element_type=jnp.float32)).astype(jnp.bfloat16)
        tmpl_re = spec_re.astype(jnp.float32)
        tmpl_im = spec_im.astype(jnp.float32)

        def one_micrograph(spectrum):
            mic_re = spectrum[0].astype(jnp.float32)
            mic_im = spectrum[1].astype(jnp.float32)
            prod_re = (mic_re * tmpl_re + mic_im * tmpl_im).astype(jnp.bfloat16)
            prod_im = (mic_im * tmpl_re - mic_re * tmpl_im).astype(jnp.bfloat16)
            part_re = jnp.dot(prod_re, cos_e, preferred_element_type=jnp.float32) - jnp.dot(prod_im, sin_e, preferred_element_type=jnp.float32)
            part_im = jnp.dot(prod_re, sin_e, preferred_element_type=jnp.float32) + jnp.dot(prod_im, cos_e, preferred_element_type=jnp.float32)
            column = jnp.dot(cos_c, part_re, precision=lax.Precision.HIGHEST) - jnp.dot(sin_c, part_im, precision=lax.Precision.HIGHEST)
            return column * factor
        return lax.map(one_micrograph, spectra)

    def accumulate(carry, template):
        corr = one_orientation(template)
        return ((jnp.maximum(carry[0], corr), carry[1] + corr * corr), None)
    start_peak = jnp.full((MICS, NFFT, WCOLS), -1e+30, jnp.float32)
    start_power = jnp.zeros((MICS, NFFT, WCOLS), jnp.float32)
    totals, unused = lax.scan(accumulate, (start_peak, start_power), templates)
    reversal = np.array([reverse_bits(place, sections) for place in range(RBANDS)], dtype=np.int32)

    def arrange(field):
        shaped = field.reshape(MICS, YB, RBANDS, WCOLS).transpose(0, 2, 1, 3)
        return shaped[:, reversal]
    return (arrange(totals[0]), arrange(totals[1]))
```

```python
import functools
import math

import jax
import jax.numpy as jnp
import numpy as np
from jax import lax
from jax.experimental import pallas as pl
from jax.experimental.pallas import tpu as pltpu
from jax.sharding import PartitionSpec as P

WCOLS = 128
MESH = pl.DeviceIdType.MESH
BLK = 16


two_pi = 2.0 * math.pi


def swapped(shard, axis, apart):
    return lax.ppermute(shard, axis, [(i, i ^ 1 << apart) for i in range(lax.axis_size(axis))])


def merged_2(part, axis, combine):
    gathered = jax.tree.map(lambda a: lax.all_gather(a, axis), part)

    def take(source):
        return jax.tree.map(lambda a: lax.dynamic_index_in_dim(a, source, 0, False), gathered)

    return lax.fori_loop(
        1, lax.axis_size(axis), lambda source, state: combine(state, take(source)), take(0)
    )


def phase_table(row_start, row_count, col_start, col_count, period):
    row_ids = row_start + jnp.arange(row_count, dtype=jnp.int32)
    col_ids = col_start + jnp.arange(col_count, dtype=jnp.int32)
    wrapped = row_ids[:, None] * col_ids[None, :] % period
    angles = wrapped.astype(jnp.float32) * (two_pi / period)
    return (jnp.cos(angles), jnp.sin(angles))


def normalize(picture):
    values = picture.astype(jnp.float32)
    centred = values - jnp.mean(values)
    factor = lax.rsqrt(jnp.mean(centred * centred) + 1e-06)
    return (centred * factor).astype(jnp.bfloat16)


def reverse_bits(number, digits):
    result = number * 0
    for digit in range(digits):
        result = result + number // (1 << digit) % 2 * (1 << digits - 1 - digit)
    return result


def combine_maps(first_pair, second_pair):
    return (jnp.maximum(first_pair[0], second_pair[0]), first_pair[1] + second_pair[1])


def shards_general(spectra, bank, orient_index):
    mic_count = spectra.shape[0]
    band_rows = spectra.shape[2]
    length = spectra.shape[3]
    tsize_px = bank.shape[1]
    row_devices = lax.axis_size("row")
    row_place = lax.axis_index("row")
    share_count = orient_index.shape[0] // lax.axis_size("orient")
    chosen = lax.dynamic_slice_in_dim(
        orient_index, lax.axis_index("orient") * share_count, share_count
    )
    templates = jax.vmap(normalize)(bank[chosen])
    cos_y, sin_y = phase_table(row_place * band_rows, band_rows, 0, tsize_px, length)
    left_table = jnp.concatenate([cos_y.astype(jnp.bfloat16), -sin_y.astype(jnp.bfloat16)], 0)
    rowpass = jnp.einsum(
        "ay,oyx->oax", left_table, templates, preferred_element_type=jnp.float32
    ).astype(jnp.bfloat16)
    cos_x, sin_x = phase_table(0, tsize_px, 0, length, length)
    right_table = jnp.concatenate([cos_x.astype(jnp.bfloat16), sin_x.astype(jnp.bfloat16)], 1)
    mixed = jnp.einsum("oax,xk->oak", rowpass, right_table, preferred_element_type=jnp.float32)
    upper_rows = mixed[:, :band_rows]
    lower_rows = mixed[:, band_rows:]
    spec_re = upper_rows[:, :, :length] + lower_rows[:, :, length:]
    spec_im = lower_rows[:, :, :length] - upper_rows[:, :, length:]
    piece = jnp.stack([spec_re, spec_im], 1).astype(jnp.bfloat16)
    cos_e, sin_e = phase_table(0, length, 0, WCOLS, length)
    row_table = jnp.concatenate([cos_e.astype(jnp.bfloat16), sin_e.astype(jnp.bfloat16)], 1)
    updates = []
    for orient_pos in range(share_count):
        tmpl_re = piece[orient_pos, 0].astype(jnp.float32)
        tmpl_im = piece[orient_pos, 1].astype(jnp.float32)
        mic_re = spectra[:, 0].astype(jnp.float32)
        mic_im = spectra[:, 1].astype(jnp.float32)
        prod_re = mic_re * tmpl_re + mic_im * tmpl_im
        prod_im = mic_im * tmpl_re - mic_re * tmpl_im
        product = jnp.stack([prod_re, prod_im], 1).astype(jnp.bfloat16)
        summed = jnp.einsum("mcbk,kw->mcbw", product, row_table, preferred_element_type=jnp.float32)
        part_re = summed[:, 0, :, :WCOLS] - summed[:, 1, :, WCOLS:]
        part_im = summed[:, 0, :, WCOLS:] + summed[:, 1, :, :WCOLS]
        updates.append(jnp.stack([part_re, part_im], 1))
    partial_value = jnp.stack(updates, 1)
    item_total = mic_count * share_count
    values = partial_value.reshape(item_total, 2, band_rows, WCOLS)
    sections = row_devices.bit_length() - 1
    for bit in reversed(range(sections)):
        half_span = 1 << bit
        partner = swapped(values, "row", bit)
        upper_side = row_place // half_span % 2
        offset = row_place % half_span
        twist = offset.astype(jnp.float32) * (math.pi / half_span)
        twist_re = jnp.cos(twist)
        twist_im = jnp.sin(twist)
        differ = partner - values
        rot_re = differ[:, 0] * twist_re - differ[:, 1] * twist_im
        rot_im = differ[:, 0] * twist_im + differ[:, 1] * twist_re
        rotated = jnp.stack([rot_re, rot_im], 1)
        values = jnp.where(upper_side == 1, rotated, values + partner)
    residue = reverse_bits(row_place, sections)
    pixel_rows = residue + row_devices * jnp.arange(band_rows, dtype=jnp.int32)
    local_rows = jnp.arange(band_rows, dtype=jnp.int32)
    wrapped_col = pixel_rows[:, None] * local_rows[None, :] % length
    col_angles = wrapped_col.astype(jnp.float32) * (two_pi / length)
    column_table = jnp.stack([jnp.cos(col_angles), -jnp.sin(col_angles)], 1)
    corr = jnp.einsum("tcj,icjw->itw", column_table, values, precision=lax.Precision.HIGHEST)
    corr = corr * (1.0 / (length * tsize_px))
    corr = corr.reshape(mic_count, share_count, band_rows, WCOLS)
    peak_part = jnp.max(corr, axis=1)
    power_part = jnp.sum(corr * corr, axis=1)
    merged = merged_2((peak_part, power_part), "orient", combine_maps)
    return (merged[0][:, None], merged[1][:, None])


def factors(rows, cols, period, shift=None):
    angle = np.outer(rows, cols) % period * (two_pi / period)
    if shift is not None:
        angle = angle + shift
    return np.stack([np.cos(angle), np.sin(angle)]).astype(np.float32)


def fused_kernel(
    sizes,
    index_ref, spectra_ref, bank_ref,
    left_a, left_b, tx_a, tx_b, te_a, te_b, col_a, col_b, tw_a, tw_b,
    peak_ref, power_ref,
    spec, left, table_x, table_e, col_hi, col_lo, twc, tws,
    rows_in, acc, send, recv, v_hi, v_lo, peak, power,
    own, sibling, merged, final,
    spec_sem, send_sem, recv_sem, pair_send, pair_recv,
    map_send, map_recv, fwd_send, fwd_recv,
):
    bands, share, band, length, tsize = sizes
    half = WCOLS // 2
    me = lax.axis_index("row")
    core = lax.axis_index("orient")

    barrier = pltpu.get_barrier_semaphore()
    for k in range(1, bands):
        pl.semaphore_signal(
            barrier, inc=1, device_id={"row": lax.rem(me + k, bands)}, device_id_type=MESH
        )
    pl.semaphore_signal(barrier, inc=1, device_id={"orient": 1 - core}, device_id_type=MESH)

    load = pltpu.make_async_copy(spectra_ref, spec, spec_sem)
    load.start()

    def rows_of(block):
        return pl.ds(pl.multiple_of(block * BLK, BLK), BLK)

    def left_body(a, carry):
        row = me * (band // BLK) + a
        ca, sa = left_a[0, pl.ds(row, 1), :], left_a[1, pl.ds(row, 1), :]
        cb, sb = left_b[0], left_b[1]
        left[0, rows_of(a), :] = (ca * cb - sa * sb).astype(jnp.bfloat16)
        left[1, rows_of(a), :] = (-(sa * cb + ca * sb)).astype(jnp.bfloat16)
        return carry

    lax.fori_loop(0, band // BLK, left_body, 0)

    def tx_body(a, carry):
        ca, sa = tx_a[0, pl.ds(a, 1), :], tx_a[1, pl.ds(a, 1), :]
        cb, sb = tx_b[0], tx_b[1]
        table_x[rows_of(a), :] = (ca * cb - sa * sb).astype(jnp.bfloat16)
        table_x[rows_of(a + tsize // BLK), :] = (sa * cb + ca * sb).astype(jnp.bfloat16)
        return carry

    lax.fori_loop(0, tsize // BLK, tx_body, 0)

    def te_body(a, carry):
        ca, sa = te_a[0, pl.ds(a, 1), :], te_a[1, pl.ds(a, 1), :]
        for part in range(2):
            cb, sb = te_b[part, 0], te_b[part, 1]
            table_e[part, rows_of(a), :] = (ca * cb - sa * sb).astype(jnp.bfloat16)
        return carry

    lax.fori_loop(0, length // BLK, te_body, 0)

    def col_body(a, carry):
        ca, sa = col_a[0, pl.ds(a, 1), :], col_a[1, pl.ds(a, 1), :]
        value = ca * col_b[0] - sa * col_b[1]
        high = value.astype(jnp.bfloat16)
        col_hi[rows_of(a), :] = high
        col_lo[rows_of(a), :] = (value - high.astype(jnp.float32)).astype(jnp.bfloat16)
        ta, ua = tw_a[0, pl.ds(a, 1), :], tw_a[1, pl.ds(a, 1), :]
        tb, ub = tw_b[0], tw_b[1]
        lane = lax.broadcasted_iota(jnp.int32, (BLK, 3 * WCOLS), 1) % WCOLS
        twc[rows_of(a), :] = ta * tb - ua * ub
        sine = ua * tb + ta * ub
        tws[rows_of(a), :] = jnp.where(lane < half, -sine, sine)
        return carry

    lax.fori_loop(0, band // BLK, col_body, 0)

    pl.semaphore_wait(barrier, bands)
    load.wait()

    kt = 256

    def orient_body(o, carry):
        picture = bank_ref[index_ref[core * share + o]].astype(jnp.float32)
        centred = picture - jnp.mean(picture)
        scale = lax.rsqrt(jnp.mean(centred * centred) + 1e-06)
        template = (centred * scale).astype(jnp.bfloat16)
        pass_re = jnp.dot(left[0], template, preferred_element_type=jnp.float32)
        pass_im = jnp.dot(left[1], template, preferred_element_type=jnp.float32)
        pass_re = pass_re.astype(jnp.bfloat16)
        pass_im = pass_im.astype(jnp.bfloat16)
        rows_in[0, :, pl.ds(0, tsize)] = pass_re
        rows_in[0, :, pl.ds(tsize, tsize)] = pass_im
        rows_in[1, :, pl.ds(0, tsize)] = pass_im
        rows_in[1, :, pl.ds(tsize, tsize)] = -pass_re
        acc[...] = jnp.zeros_like(acc)

        def kx_body(k, inner):
            cols = pl.ds(pl.multiple_of(k * kt, kt), kt)
            wide = table_x[:, cols]
            t_re = jnp.dot(rows_in[0], wide, preferred_element_type=jnp.float32)
            t_im = jnp.dot(rows_in[1], wide, preferred_element_type=jnp.float32)
            t_re = t_re.astype(jnp.bfloat16).astype(jnp.float32)
            t_im = t_im.astype(jnp.bfloat16).astype(jnp.float32)
            for m in range(2):
                m_re = spec[m, 0, :, cols].astype(jnp.float32)
                m_im = spec[m, 1, :, cols].astype(jnp.float32)
                p_re = (m_re * t_re + m_im * t_im).astype(jnp.bfloat16)
                p_im = (m_im * t_re - m_re * t_im).astype(jnp.bfloat16)
                acc[m] += jnp.dot(
                    p_re, table_e[0, cols, :], preferred_element_type=jnp.float32
                ) + jnp.dot(p_im, table_e[1, cols, :], preferred_element_type=jnp.float32)
            return inner

        lax.fori_loop(0, length // kt, kx_body, 0)
        for d in range(bands):
            tile = acc[d // 2, :, pl.ds(d % 2 * WCOLS, WCOLS)].astype(jnp.bfloat16)

            @pl.when(me == d)
            def _():
                recv[me, o] = tile

            @pl.when(me != d)
            def _():
                send[d, o] = tile

        for k in (2, 1, 3):
            dest = lax.rem(me + k, bands)
            pltpu.make_async_remote_copy(
                src_ref=send.at[dest, o], dst_ref=recv.at[me, o],
                send_sem=send_sem.at[k, o], recv_sem=recv_sem.at[me, o],
                device_id={"row": dest}, device_id_type=MESH,
            ).start()
        return carry

    lax.fori_loop(0, share, orient_body, 0)

    peak[...] = jnp.full_like(peak, -1e30)
    power[...] = jnp.zeros_like(power)
    factor = 1.0 / (length * tsize)
    rc = 64

    def column_body(o, carry):
        for k in range(1, bands):
            source = lax.rem(me + k, bands)
            pltpu.make_async_remote_copy(
                src_ref=send.at[source, o], dst_ref=recv.at[source, o],
                send_sem=send_sem.at[k, o], recv_sem=recv_sem.at[source, o],
                device_id={"row": source}, device_id_type=MESH,
            ).wait_recv()

        def chunk(c, inner):
            rows = pl.ds(pl.multiple_of(c * rc, rc), rc)
            lane = lax.broadcasted_iota(jnp.int32, (rc, WCOLS), 1)
            first = lane < half
            b0, b1, b2, b3 = [recv[b, o, rows, :].astype(jnp.float32) for b in range(4)]
            s02, d02, s13, d13 = b0 + b2, b0 - b2, b1 + b3, b1 - b3
            turned = pltpu.roll(d13, half, 1)
            turned = jnp.where(first, -turned, turned)
            u = [s02 + s13, d02 + turned, s02 - s13, d02 - turned]
            v = [u[0]]
            for rho in range(1, 4):
                span = pl.ds((rho - 1) * WCOLS, WCOLS)
                v.append(u[rho] * twc[rows, span] + pltpu.roll(u[rho], half, 1) * tws[rows, span])
            for pair in range(2):
                even, odd = v[2 * pair], v[2 * pair + 1]
                v_re = jnp.where(first, even, pltpu.roll(odd, half, 1))
                v_im = jnp.where(first, pltpu.roll(even, half, 1), odd)
                span = pl.ds(pair * WCOLS, WCOLS)
                for part, value in enumerate((v_re, v_im)):
                    high = value.astype(jnp.bfloat16)
                    where = pl.ds(pl.multiple_of(part * band + c * rc, rc), rc)
                    v_hi[where, span] = high
                    v_lo[where, span] = (value - high.astype(jnp.float32)).astype(jnp.bfloat16)
            return inner

        lax.fori_loop(0, band // rc, chunk, 0)
        corr = jnp.dot(col_hi[...], v_hi[...], preferred_element_type=jnp.float32)
        corr += jnp.dot(col_lo[...], v_hi[...], preferred_element_type=jnp.float32)
        corr += jnp.dot(col_hi[...], v_lo[...], preferred_element_type=jnp.float32)
        corr = corr * factor
        peak[...] = jnp.maximum(peak[...], corr)
        power[...] += corr * corr
        return carry

    lax.fori_loop(0, share, column_body, 0)

    first = lax.broadcasted_iota(jnp.int32, (band, WCOLS), 1) < half
    for q in range(4):
        rho = (q % 2) * 2 + q // 2
        span = pl.ds(rho // 2 * WCOLS, WCOLS)
        hi, po = peak[:, span], power[:, span]
        if rho % 2 == 0:
            own[q] = jnp.where(first, hi, pltpu.roll(po, half, 1))
        else:
            own[q] = jnp.where(first, pltpu.roll(hi, half, 1), po)

    hb = band // 2
    mine = pl.ds(pl.multiple_of(core * hb, hb), hb)
    theirs = pl.ds(pl.multiple_of((1 - core) * hb, hb), hb)
    swap = pltpu.make_async_remote_copy(
        src_ref=own.at[:, theirs, :], dst_ref=sibling,
        send_sem=pair_send, recv_sem=pair_recv,
        device_id={"orient": 1 - core}, device_id_type=MESH,
    )
    swap.start()
    swap.wait()
    first = lax.broadcasted_iota(jnp.int32, (hb, WCOLS), 1) < half
    for q in range(4):
        one, two = own[q, mine, :], sibling[q]
        total = jnp.where(first, jnp.maximum(one, two), one + two)

        @pl.when(me == q)
        def _():
            final[me, mine, :] = total

        @pl.when(me != q)
        def _():
            merged[q] = total

    def map_copy(k, source):
        dest = lax.rem(me + k, bands)
        return pltpu.make_async_remote_copy(
            src_ref=merged.at[dest], dst_ref=final.at[source, mine, :],
            send_sem=map_send.at[k], recv_sem=map_recv.at[source],
            device_id={"row": dest}, device_id_type=MESH,
        )

    def forward(source, rows):
        return pltpu.make_async_remote_copy(
            src_ref=final.at[source, rows, :], dst_ref=final.at[source, rows, :],
            send_sem=fwd_send.at[source], recv_sem=fwd_recv.at[source],
            device_id={"orient": 1 - core}, device_id_type=MESH,
        )

    for k in (2, 1, 3):
        map_copy(k, me).start()
    forward(me, mine).start()
    for k in (1, 3, 2):
        source = lax.rem(me + k, bands)
        map_copy(k, source).wait_recv()
        forward(source, mine).start()
    for source in range(4):
        forward(source, theirs).wait_recv()
    first = lax.broadcasted_iota(jnp.int32, (band, WCOLS), 1) < half
    for m in range(2):
        a, b = final[2 * m], final[2 * m + 1]
        peak_ref[m, 0] = jnp.where(first, a, pltpu.roll(b, half, 1))
        power_ref[m, 0] = jnp.where(first, pltpu.roll(a, half, 1), b)

    for source in range(4):
        forward(source, mine).wait_send()
    for k in range(1, bands):
        map_copy(k, me).wait_send()

    def drain(o, carry):
        for k in range(1, bands):
            dest = lax.rem(me + k, bands)
            pltpu.make_async_remote_copy(
                src_ref=send.at[dest, o], dst_ref=recv.at[me, o],
                send_sem=send_sem.at[k, o], recv_sem=recv_sem.at[me, o],
                device_id={"row": dest}, device_id_type=MESH,
            ).wait_send()
        return carry

    lax.fori_loop(0, share, drain, 0)


def shards_fused(spectra, bank, orient_index):
    band = spectra.shape[2]
    length = spectra.shape[3]
    tsize = bank.shape[1]
    bands = lax.axis_size("row")
    share = orient_index.shape[0] // lax.axis_size("orient")
    half = WCOLS // 2
    bf, f32 = jnp.bfloat16, jnp.float32

    small = np.arange(BLK)
    y = np.arange(tsize)
    kx = np.arange(length)
    lane = np.arange(2 * WCOLS)
    lane_x = lane // WCOLS * half + lane % half
    is_im = lane % WCOLS >= half
    quarter = two_pi / 4
    te_b = np.stack(
        [
            factors(small, lane_x, length, np.where(is_im, -quarter, 0.0)),
            factors(small, lane_x, length, np.where(is_im, 0.0, quarter)),
        ]
    )
    j = np.arange(band)
    col_j = np.concatenate([j, j])
    col_shift = np.where(np.arange(2 * band) < band, 0.0, quarter)
    rho = np.repeat(np.arange(1, 4), WCOLS)
    tables = [
        factors(np.arange(length // BLK) * BLK, y, length),
        factors(small, y, length),
        factors(np.arange(tsize // BLK) * BLK, kx, length),
        factors(small, kx, length),
        factors(np.arange(length // BLK) * BLK, lane_x, length),
        te_b,
        factors(np.arange(band // BLK) * BLK, col_j, band),
        factors(small, col_j, band, col_shift),
        factors(np.arange(band // BLK) * BLK, rho, length),
        factors(small, rho, length),
    ]
    out = jax.ShapeDtypeStruct((2, 1, band, WCOLS), f32)
    vmem = pl.BlockSpec(memory_space=pltpu.VMEM)
    dma = pltpu.SemaphoreType.DMA
    return pl.pallas_call(
        functools.partial(fused_kernel, (bands, share, band, length, tsize)),
        out_shape=(out, out),
        in_specs=[
            pl.BlockSpec(memory_space=pltpu.SMEM),
            pl.BlockSpec(memory_space=pl.ANY),
        ]
        + [vmem] * (1 + len(tables)),
        out_specs=(vmem, vmem),
        scratch_shapes=[
            pltpu.VMEM((2, 2, band, length), bf),
            pltpu.VMEM((2, band, tsize), bf),
            pltpu.VMEM((2 * tsize, length), bf),
            pltpu.VMEM((2, length, 2 * WCOLS), bf),
            pltpu.VMEM((band, 2 * band), bf),
            pltpu.VMEM((band, 2 * band), bf),
            pltpu.VMEM((band, 3 * WCOLS), f32),
            pltpu.VMEM((band, 3 * WCOLS), f32),
            pltpu.VMEM((2, band, 2 * tsize), bf),
            pltpu.VMEM((2, band, 2 * WCOLS), f32),
            pltpu.VMEM((bands, share, band, WCOLS), bf),
            pltpu.VMEM((bands, share, band, WCOLS), bf),
            pltpu.VMEM((2 * band, 2 * WCOLS), bf),
            pltpu.VMEM((2 * band, 2 * WCOLS), bf),
            pltpu.VMEM((band, 2 * WCOLS), f32),
            pltpu.VMEM((band, 2 * WCOLS), f32),
            pltpu.VMEM((4, band, WCOLS), f32),
            pltpu.VMEM((4, band // 2, WCOLS), f32),
            pltpu.VMEM((4, band // 2, WCOLS), f32),
            pltpu.VMEM((4, band, WCOLS), f32),
            dma,
            dma((bands, share)),
            dma((bands, share)),
            dma,
            dma,
            dma((bands,)),
            dma((bands,)),
            dma((bands,)),
            dma((bands,)),
        ],
        compiler_params=pltpu.CompilerParams(
            collective_id=0, has_side_effects=True, vmem_limit_bytes=60 << 20
        ),
    )(orient_index, spectra, bank, *tables)


def shards(spectra, bank, orient_index):
    fits = (
        lax.axis_size("row") == 4
        and lax.axis_size("orient") == 2
        and spectra.shape[0] == 2
        and spectra.shape[2] % 128 == 0
        and spectra.shape[3] == 4 * spectra.shape[2]
    )
    body = shards_fused if fits else shards_general
    return body(spectra, bank, orient_index)


def solution(mesh):
    return jax.shard_map(
        shards,
        mesh=mesh,
        in_specs=(P(("grp", "mic"), None, "row", None), P(), P("grp")),
        out_specs=(P(("grp", "mic"), "row", None, None), P(("grp", "mic"), "row", None, None)),
        check_vma=False,
    )
```

```python
import functools
import math

import jax
import jax.numpy as jnp
import numpy as np
from jax import lax
from jax.experimental import pallas as pl
from jax.experimental.pallas import tpu as pltpu
from jax.sharding import PartitionSpec as P

WCOLS = 128
MESH = pl.DeviceIdType.MESH
BLK = 16
PRODUCT = jnp.float32
MAPS = jnp.bfloat16


two_pi = 2.0 * math.pi


def swapped(shard, axis, apart):
    return lax.ppermute(shard, axis, [(i, i ^ 1 << apart) for i in range(lax.axis_size(axis))])


def merged_2(part, axis, combine):
    gathered = jax.tree.map(lambda a: lax.all_gather(a, axis), part)

    def take(source):
        return jax.tree.map(lambda a: lax.dynamic_index_in_dim(a, source, 0, False), gathered)

    return lax.fori_loop(
        1, lax.axis_size(axis), lambda source, state: combine(state, take(source)), take(0)
    )


def phase_table(row_start, row_count, col_start, col_count, period):
    row_ids = row_start + jnp.arange(row_count, dtype=jnp.int32)
    col_ids = col_start + jnp.arange(col_count, dtype=jnp.int32)
    wrapped = row_ids[:, None] * col_ids[None, :] % period
    angles = wrapped.astype(jnp.float32) * (two_pi / period)
    return (jnp.cos(angles), jnp.sin(angles))


def normalize(picture):
    values = picture.astype(jnp.float32)
    centred = values - jnp.mean(values)
    factor = lax.rsqrt(jnp.mean(centred * centred) + 1e-06)
    return (centred * factor).astype(jnp.bfloat16)


def reverse_bits(number, digits):
    result = number * 0
    for digit in range(digits):
        result = result + number // (1 << digit) % 2 * (1 << digits - 1 - digit)
    return result


def combine_maps(first_pair, second_pair):
    return (jnp.maximum(first_pair[0], second_pair[0]), first_pair[1] + second_pair[1])


def shards_general(spectra, bank, orient_index):
    mic_count = spectra.shape[0]
    band_rows = spectra.shape[2]
    length = spectra.shape[3]
    tsize_px = bank.shape[1]
    row_devices = lax.axis_size("row")
    row_place = lax.axis_index("row")
    share_count = orient_index.shape[0] // lax.axis_size("orient")
    chosen = lax.dynamic_slice_in_dim(
        orient_index, lax.axis_index("orient") * share_count, share_count
    )
    templates = jax.vmap(normalize)(bank[chosen])
    cos_y, sin_y = phase_table(row_place * band_rows, band_rows, 0, tsize_px, length)
    left_table = jnp.concatenate([cos_y.astype(jnp.bfloat16), -sin_y.astype(jnp.bfloat16)], 0)
    rowpass = jnp.einsum(
        "ay,oyx->oax", left_table, templates, preferred_element_type=jnp.float32
    ).astype(jnp.bfloat16)
    cos_x, sin_x = phase_table(0, tsize_px, 0, length, length)
    right_table = jnp.concatenate([cos_x.astype(jnp.bfloat16), sin_x.astype(jnp.bfloat16)], 1)
    mixed = jnp.einsum("oax,xk->oak", rowpass, right_table, preferred_element_type=jnp.float32)
    upper_rows = mixed[:, :band_rows]
    lower_rows = mixed[:, band_rows:]
    spec_re = upper_rows[:, :, :length] + lower_rows[:, :, length:]
    spec_im = lower_rows[:, :, :length] - upper_rows[:, :, length:]
    piece = jnp.stack([spec_re, spec_im], 1).astype(jnp.bfloat16)
    cos_e, sin_e = phase_table(0, length, 0, WCOLS, length)
    row_table = jnp.concatenate([cos_e.astype(jnp.bfloat16), sin_e.astype(jnp.bfloat16)], 1)
    updates = []
    for orient_pos in range(share_count):
        tmpl_re = piece[orient_pos, 0].astype(jnp.float32)
        tmpl_im = piece[orient_pos, 1].astype(jnp.float32)
        mic_re = spectra[:, 0].astype(jnp.float32)
        mic_im = spectra[:, 1].astype(jnp.float32)
        prod_re = mic_re * tmpl_re + mic_im * tmpl_im
        prod_im = mic_im * tmpl_re - mic_re * tmpl_im
        product = jnp.stack([prod_re, prod_im], 1).astype(jnp.bfloat16)
        summed = jnp.einsum("mcbk,kw->mcbw", product, row_table, preferred_element_type=jnp.float32)
        part_re = summed[:, 0, :, :WCOLS] - summed[:, 1, :, WCOLS:]
        part_im = summed[:, 0, :, WCOLS:] + summed[:, 1, :, :WCOLS]
        updates.append(jnp.stack([part_re, part_im], 1))
    partial_value = jnp.stack(updates, 1)
    item_total = mic_count * share_count
    values = partial_value.reshape(item_total, 2, band_rows, WCOLS)
    sections = row_devices.bit_length() - 1
    for bit in reversed(range(sections)):
        half_span = 1 << bit
        partner = swapped(values, "row", bit)
        upper_side = row_place // half_span % 2
        offset = row_place % half_span
        twist = offset.astype(jnp.float32) * (math.pi / half_span)
        twist_re = jnp.cos(twist)
        twist_im = jnp.sin(twist)
        differ = partner - values
        rot_re = differ[:, 0] * twist_re - differ[:, 1] * twist_im
        rot_im = differ[:, 0] * twist_im + differ[:, 1] * twist_re
        rotated = jnp.stack([rot_re, rot_im], 1)
        values = jnp.where(upper_side == 1, rotated, values + partner)
    residue = reverse_bits(row_place, sections)
    pixel_rows = residue + row_devices * jnp.arange(band_rows, dtype=jnp.int32)
    local_rows = jnp.arange(band_rows, dtype=jnp.int32)
    wrapped_col = pixel_rows[:, None] * local_rows[None, :] % length
    col_angles = wrapped_col.astype(jnp.float32) * (two_pi / length)
    column_table = jnp.stack([jnp.cos(col_angles), -jnp.sin(col_angles)], 1)
    corr = jnp.einsum("tcj,icjw->itw", column_table, values, precision=lax.Precision.HIGHEST)
    corr = corr * (1.0 / (length * tsize_px))
    corr = corr.reshape(mic_count, share_count, band_rows, WCOLS)
    peak_part = jnp.max(corr, axis=1)
    power_part = jnp.sum(corr * corr, axis=1)
    merged = merged_2((peak_part, power_part), "orient", combine_maps)
    return (merged[0][:, None], merged[1][:, None])


def factors(rows, cols, period, shift=None):
    angle = np.outer(rows, cols) % period * (two_pi / period)
    if shift is not None:
        angle = angle + shift
    return np.stack([np.cos(angle), np.sin(angle)]).astype(np.float32)


def fused_kernel(
    sizes,
    index_ref, spectra_ref, bank_ref, w384, w512, w256, w1024,
    final,
    spec, bank, f384, f512, f256, f1024,
    left, table_x, table_e, col_hi, col_lo, twc, tws, order,
    rows_in, prod, send, recv, v_hi, v_lo, peak, power,
    own, sibling, merged,
    load_sem, send_sem, recv_sem, pair_send, pair_recv,
    map_send, map_recv, fwd_send, fwd_recv,
):
    bands, share, band, length, tsize = sizes
    half = WCOLS // 2
    hb = band // 2
    kq = length // 4
    me = lax.axis_index("row")
    core = lax.axis_index("orient")

    loads = [
        pltpu.make_async_copy(source, target, load_sem.at[n])
        for n, (source, target) in enumerate(
            [(w384, f384), (w512, f512), (w256, f256), (w1024, f1024), (bank_ref, bank), (spectra_ref, spec)]
        )
    ]
    for load in loads:
        load.start()
    barrier = pltpu.get_barrier_semaphore()
    for k in range(1, bands):
        pl.semaphore_signal(
            barrier, inc=1, device_id={"row": lax.rem(me + k, bands)}, device_id_type=MESH
        )
    pl.semaphore_signal(barrier, inc=1, device_id={"orient": 1 - core}, device_id_type=MESH)

    def rows_of(block):
        return pl.ds(pl.multiple_of(block * BLK, BLK), BLK)

    at = lax.broadcasted_iota(jnp.int32, (tsize, 4 * WCOLS), 1)
    x = lax.broadcasted_iota(jnp.int32, (tsize, 4 * WCOLS), 0)
    picked = (x == 4 * (at % WCOLS) + at // WCOLS) & (at % WCOLS < tsize // 4)
    order[...] = jnp.where(picked, 1.0, 0.0).astype(jnp.bfloat16)

    loads[0].wait()
    n_left = length // BLK

    def left_body(a, carry):
        row = me * (band // BLK) + a
        ca, sa = f384[0, pl.ds(row, 1), :], f384[1, pl.ds(row, 1), :]
        cb, sb = f384[0, pl.ds(n_left, BLK), :], f384[1, pl.ds(n_left, BLK), :]
        left[0, rows_of(a), :] = (ca * cb - sa * sb).astype(jnp.bfloat16)
        left[1, rows_of(a), :] = (-(sa * cb + ca * sb)).astype(jnp.bfloat16)
        return carry

    lax.fori_loop(0, band // BLK, left_body, 0)
    loads[1].wait()

    def tx_body(a, carry):
        ca, sa = f512[0, pl.ds(a, 1), :], f512[1, pl.ds(a, 1), :]
        for s in range(4):
            where = pl.ds((s + 1) * BLK, BLK)
            cb, sb = f512[0, where, :], f512[1, where, :]
            table_x[s, rows_of(a), :] = (ca * cb - sa * sb).astype(jnp.bfloat16)
            table_x[s, rows_of(a + WCOLS // BLK), :] = (sa * cb + ca * sb).astype(jnp.bfloat16)
        return carry

    lax.fori_loop(0, WCOLS // BLK, tx_body, 0)
    loads[2].wait()
    ft = kq // 2

    def te_body(a, carry):
        ca, sa = f256[0, pl.ds(a, 1), :], f256[1, pl.ds(a, 1), :]
        per = ft // BLK
        tile, u, block = a // per % 2, a // (2 * per), a % per
        for part in range(2):
            where = pl.ds(n_left + part * BLK, BLK)
            cb, sb = f256[0, where, :], f256[1, where, :]
            row = (part * 4 + u) * ft + block * BLK
            table_e[tile, pl.ds(pl.multiple_of(row, BLK), BLK), :] = (ca * cb - sa * sb).astype(
                jnp.bfloat16
            )
        return carry

    lax.fori_loop(0, length // BLK, te_body, 0)
    pl.semaphore_wait(barrier, bands)
    loads[4].wait()
    loads[5].wait()

    def orient_body(o, carry):
        picture = bank[index_ref[core * share + o]].astype(jnp.float32)
        centred = picture - jnp.mean(picture)
        scale = lax.rsqrt(jnp.mean(centred * centred) + 1e-06)
        template = (centred * scale).astype(jnp.bfloat16)
        template = jnp.dot(template, order[...], preferred_element_type=jnp.float32)
        template = template.astype(jnp.bfloat16)
        for n in range(2):
            value = jnp.dot(left[n], template, preferred_element_type=jnp.float32)
            value = value.astype(jnp.bfloat16)
            for s in range(4):
                piece = value[:, s * WCOLS : (s + 1) * WCOLS]
                if n == 0:
                    rows_in[s, 0, :, pl.ds(0, WCOLS)] = piece
                    rows_in[s, 1, :, pl.ds(WCOLS, WCOLS)] = -piece
                else:
                    rows_in[s, 0, :, pl.ds(WCOLS, WCOLS)] = piece
                    rows_in[s, 1, :, pl.ds(0, WCOLS)] = piece

        def half_body(h, inner):
            rows = pl.ds(pl.multiple_of(h * hb, hb), hb)
            total = None
            for tile in range(2):
                cols = pl.ds(tile * ft, ft)
                re, im = [], []
                for s in range(4):
                    wide = table_x[s, :, cols]
                    re.append(jnp.dot(rows_in[s, 0, rows, :], wide, preferred_element_type=jnp.float32))
                    im.append(jnp.dot(rows_in[s, 1, rows, :], wide, preferred_element_type=jnp.float32))
                s02r, d02r, s13r, d13r = re[0] + re[2], re[0] - re[2], re[1] + re[3], re[1] - re[3]
                s02i, d02i, s13i, d13i = im[0] + im[2], im[0] - im[2], im[1] + im[3], im[1] - im[3]
                quads = [
                    (s02r + s13r, s02i + s13i),
                    (d02r + d13i, d02i - d13r),
                    (s02r - s13r, s02i - s13i),
                    (d02r - d13i, d02i + d13r),
                ]
                for u, (t_re, t_im) in enumerate(quads):
                    t_re = t_re.astype(jnp.bfloat16).astype(PRODUCT)
                    t_im = t_im.astype(jnp.bfloat16).astype(PRODUCT)
                    where = pl.ds(u * kq + tile * ft, ft)
                    for m in range(2):
                        m_re = spec[m, 0, rows, where].astype(PRODUCT)
                        m_im = spec[m, 1, rows, where].astype(PRODUCT)
                        p_re = (m_re * t_re + m_im * t_im).astype(jnp.bfloat16)
                        p_im = (m_im * t_re - m_re * t_im).astype(jnp.bfloat16)
                        prod[tile, pl.ds(m * hb, hb), pl.ds(u * ft, ft)] = p_re
                        prod[tile, pl.ds(m * hb, hb), pl.ds((4 + u) * ft, ft)] = p_im
                value = jnp.dot(prod[tile], table_e[tile], preferred_element_type=jnp.float32)
                total = value if total is None else total + value
            total = total.astype(jnp.bfloat16)
            for d in range(bands):
                m, xh = d // 2, d % 2
                tile = total[m * hb : (m + 1) * hb, xh * WCOLS : (xh + 1) * WCOLS]

                @pl.when(me == d)
                def _():
                    recv[me, o, rows, :] = tile

                @pl.when(me != d)
                def _():
                    send[d, o, rows, :] = tile

            for k in (2, 1, 3):
                part_copy(k, lax.rem(me + k, bands), me, o, h).start()
            return inner

        lax.fori_loop(0, 2, half_body, 0)
        return carry

    def part_copy(k, dest, source, o, h):
        rows = pl.ds(pl.multiple_of(h * hb, hb), hb)
        return pltpu.make_async_remote_copy(
            src_ref=send.at[dest, o, rows, :], dst_ref=recv.at[source, o, rows, :],
            send_sem=send_sem.at[k, o, h], recv_sem=recv_sem.at[source, o, h],
            device_id={"row": dest}, device_id_type=MESH,
        )

    lax.fori_loop(0, share, orient_body, 0)
    loads[3].wait()
    n_col = band // BLK

    def col_body(a, carry):
        ca, sa = f1024[0, pl.ds(a, 1), :], f1024[1, pl.ds(a, 1), :]
        value = ca * f1024[0, pl.ds(n_col, BLK), :] - sa * f1024[1, pl.ds(n_col, BLK), :]
        high = value.astype(jnp.bfloat16)
        col_hi[rows_of(a), :] = high
        col_lo[rows_of(a), :] = (value - high.astype(jnp.float32)).astype(jnp.bfloat16)
        base = n_left + BLK
        ta, ua = f384[0, pl.ds(base + a, 1), :], f384[1, pl.ds(base + a, 1), :]
        where = pl.ds(base + n_col, BLK)
        tb, ub = f384[0, where, :], f384[1, where, :]
        lane = lax.broadcasted_iota(jnp.int32, (BLK, 3 * WCOLS), 1) % WCOLS
        twc[rows_of(a), :] = ta * tb - ua * ub
        sine = ua * tb + ta * ub
        tws[rows_of(a), :] = jnp.where(lane < half, -sine, sine)
        return carry

    lax.fori_loop(0, band // BLK, col_body, 0)

    peak[...] = jnp.full_like(peak, -1e30)
    power[...] = jnp.zeros_like(power)
    factor = 1.0 / (length * tsize)
    rc = 64

    def column_body(o, carry):
        for k in range(1, bands):
            source = lax.rem(me + k, bands)
            for h in range(2):
                part_copy(k, source, source, o, h).wait_recv()

        def chunk(c, inner):
            rows = pl.ds(pl.multiple_of(c * rc, rc), rc)
            lane = lax.broadcasted_iota(jnp.int32, (rc, WCOLS), 1)
            first = lane < half
            b0, b1, b2, b3 = [recv[b, o, rows, :].astype(jnp.float32) for b in range(4)]
            s02, d02, s13, d13 = b0 + b2, b0 - b2, b1 + b3, b1 - b3
            turned = pltpu.roll(d13, half, 1)
            turned = jnp.where(first, -turned, turned)
            u = [s02 + s13, d02 + turned, s02 - s13, d02 - turned]
            v = [u[0]]
            for rho in range(1, 4):
                span = pl.ds((rho - 1) * WCOLS, WCOLS)
                v.append(u[rho] * twc[rows, span] + pltpu.roll(u[rho], half, 1) * tws[rows, span])
            for pair in range(2):
                even, odd = v[2 * pair], v[2 * pair + 1]
                v_re = jnp.where(first, even, pltpu.roll(odd, half, 1))
                v_im = jnp.where(first, pltpu.roll(even, half, 1), odd)
                span = pl.ds(pair * WCOLS, WCOLS)
                for part, value in enumerate((v_re, v_im)):
                    high = value.astype(jnp.bfloat16)
                    where = pl.ds(pl.multiple_of(part * band + c * rc, rc), rc)
                    v_hi[where, span] = high
                    v_lo[where, span] = (value - high.astype(jnp.float32)).astype(jnp.bfloat16)
            return inner

        lax.fori_loop(0, band // rc, chunk, 0)
        corr = jnp.dot(col_hi[...], v_hi[...], preferred_element_type=jnp.float32)
        corr += jnp.dot(col_lo[...], v_hi[...], preferred_element_type=jnp.float32)
        corr += jnp.dot(col_hi[...], v_lo[...], preferred_element_type=jnp.float32)
        corr = corr * factor
        peak[...] = jnp.maximum(peak[...], corr)
        power[...] += corr * corr
        return carry

    lax.fori_loop(0, share, column_body, 0)

    first = lax.broadcasted_iota(jnp.int32, (band, WCOLS), 1) < half
    for q in range(4):
        rho = (q % 2) * 2 + q // 2
        span = pl.ds(rho // 2 * WCOLS, WCOLS)
        hi, po = peak[:, span], power[:, span]
        if rho % 2 == 0:
            own[q] = jnp.where(first, hi, pltpu.roll(po, half, 1))
        else:
            own[q] = jnp.where(first, pltpu.roll(hi, half, 1), po)

    mine = pl.ds(pl.multiple_of(core * hb, hb), hb)
    theirs = pl.ds(pl.multiple_of((1 - core) * hb, hb), hb)
    swap = pltpu.make_async_remote_copy(
        src_ref=own.at[:, theirs, :], dst_ref=sibling,
        send_sem=pair_send, recv_sem=pair_recv,
        device_id={"orient": 1 - core}, device_id_type=MESH,
    )
    swap.start()
    swap.wait()
    first = lax.broadcasted_iota(jnp.int32, (hb, WCOLS), 1) < half
    for q in range(4):
        one, two = own[q, mine, :], sibling[q]
        total = jnp.where(first, jnp.maximum(one, two), one + two).astype(final.dtype)

        @pl.when(me == q)
        def _():
            final[me, mine, :] = total

        @pl.when(me != q)
        def _():
            merged[q] = total

    def map_copy(k, source):
        dest = lax.rem(me + k, bands)
        return pltpu.make_async_remote_copy(
            src_ref=merged.at[dest], dst_ref=final.at[source, mine, :],
            send_sem=map_send.at[k], recv_sem=map_recv.at[source],
            device_id={"row": dest}, device_id_type=MESH,
        )

    def forward(source, rows):
        return pltpu.make_async_remote_copy(
            src_ref=final.at[source, rows, :], dst_ref=final.at[source, rows, :],
            send_sem=fwd_send.at[source], recv_sem=fwd_recv.at[source],
            device_id={"orient": 1 - core}, device_id_type=MESH,
        )

    for k in (2, 1, 3):
        map_copy(k, me).start()
    forward(me, mine).start()
    for k in (1, 3, 2):
        source = lax.rem(me + k, bands)
        map_copy(k, source).wait_recv()
        forward(source, mine).start()
    for source in range(4):
        forward(source, theirs).wait_recv()
    for source in range(4):
        forward(source, mine).wait_send()
    for k in range(1, bands):
        map_copy(k, me).wait_send()

    def drain(o, carry):
        for k in range(1, bands):
            dest = lax.rem(me + k, bands)
            for h in range(2):
                part_copy(k, dest, me, o, h).wait_send()
        return carry

    lax.fori_loop(0, share, drain, 0)


def assemble_kernel(maps, peak_ref, power_ref):
    half = WCOLS // 2
    first = lax.broadcasted_iota(jnp.int32, maps.shape[1:], 1) < half
    for m in range(2):
        a, b = maps[2 * m].astype(jnp.float32), maps[2 * m + 1].astype(jnp.float32)
        peak_ref[m, 0] = jnp.where(first, a, pltpu.roll(b, half, 1))
        power_ref[m, 0] = jnp.where(first, pltpu.roll(a, half, 1), b)


def shards_fused(spectra, bank, orient_index):
    band = spectra.shape[2]
    length = spectra.shape[3]
    tsize = bank.shape[1]
    bands = lax.axis_size("row")
    share = orient_index.shape[0] // lax.axis_size("orient")
    half = WCOLS // 2
    bf, f32 = jnp.bfloat16, jnp.float32

    small = np.arange(BLK)
    y = np.arange(tsize)
    kq = np.arange(length // 4)
    lane = np.arange(2 * WCOLS)
    lane_x = lane // WCOLS * half + lane % half
    is_im = lane % WCOLS >= half
    quarter = two_pi / 4
    steps = np.arange(length // BLK) * BLK
    short = np.arange(band // BLK) * BLK
    j = np.arange(band)
    col_j = np.concatenate([j, j])
    col_shift = np.where(np.arange(2 * band) < band, 0.0, quarter)
    rho = np.repeat(np.arange(1, 4), WCOLS)
    spread = np.concatenate([np.arange(BLK) * 4 * BLK] + [4 * small + s for s in range(4)])
    w384 = np.concatenate(
        [
            factors(steps, y, length),
            factors(small, y, length),
            factors(short, rho, length),
            factors(small, rho, length),
        ],
        1,
    )
    w512 = factors(spread, kq, length)
    w256 = np.concatenate(
        [
            factors(steps, lane_x, length),
            factors(small, lane_x, length, np.where(is_im, -quarter, 0.0)),
            factors(small, lane_x, length, np.where(is_im, 0.0, quarter)),
        ],
        1,
    )
    w1024 = np.concatenate(
        [factors(short, col_j, band), factors(small, col_j, band, col_shift)], 1
    )
    tables = [w384, w512, w256, w1024]
    vmem = pl.BlockSpec(memory_space=pltpu.VMEM)
    hbm = pl.BlockSpec(memory_space=pl.ANY)
    dma = pltpu.SemaphoreType.DMA
    maps = pl.pallas_call(
        functools.partial(fused_kernel, (bands, share, band, length, tsize)),
        out_shape=jax.ShapeDtypeStruct((4, band, WCOLS), MAPS),
        in_specs=[pl.BlockSpec(memory_space=pltpu.SMEM)] + [hbm] * (2 + len(tables)),
        out_specs=vmem,
        scratch_shapes=[
            pltpu.VMEM(spectra.shape, bf),
            pltpu.VMEM(bank.shape, bf),
        ]
        + [pltpu.VMEM(table.shape, f32) for table in tables]
        + [
            pltpu.VMEM((2, band, tsize), bf),
            pltpu.VMEM((4, 2 * WCOLS, length // 4), bf),
            pltpu.VMEM((2, length, 2 * WCOLS), bf),
            pltpu.VMEM((band, 2 * band), bf),
            pltpu.VMEM((band, 2 * band), bf),
            pltpu.VMEM((band, 3 * WCOLS), f32),
            pltpu.VMEM((band, 3 * WCOLS), f32),
            pltpu.VMEM((tsize, 4 * WCOLS), bf),
            pltpu.VMEM((4, 2, band, 2 * WCOLS), bf),
            pltpu.VMEM((2, band, length), bf),
            pltpu.VMEM((bands, share, band, WCOLS), bf),
            pltpu.VMEM((bands, share, band, WCOLS), bf),
            pltpu.VMEM((2 * band, 2 * WCOLS), bf),
            pltpu.VMEM((2 * band, 2 * WCOLS), bf),
            pltpu.VMEM((band, 2 * WCOLS), f32),
            pltpu.VMEM((band, 2 * WCOLS), f32),
            pltpu.VMEM((4, band, WCOLS), f32),
            pltpu.VMEM((4, band // 2, WCOLS), f32),
            pltpu.VMEM((4, band // 2, WCOLS), MAPS),
            dma((6,)),
            dma((bands, share, 2)),
            dma((bands, share, 2)),
            dma,
            dma,
            dma((bands,)),
            dma((bands,)),
            dma((bands,)),
            dma((bands,)),
        ],
        compiler_params=pltpu.CompilerParams(
            collective_id=0, has_side_effects=True, vmem_limit_bytes=58 << 20
        ),
    )(orient_index, spectra, bank, *tables)
    out = jax.ShapeDtypeStruct((2, 1, band, WCOLS), f32)
    return pl.pallas_call(
        assemble_kernel, out_shape=(out, out), in_specs=[vmem], out_specs=(vmem, vmem)
    )(maps)


def shards(spectra, bank, orient_index):
    fits = (
        lax.axis_size("row") == 4
        and lax.axis_size("orient") == 2
        and spectra.shape[0] == 2
        and spectra.shape[2] % 128 == 0
        and bank.shape[1] == 3 * WCOLS
        and spectra.shape[3] == 4 * spectra.shape[2]
    )
    body = shards_fused if fits else shards_general
    return body(spectra, bank, orient_index)


def solution(mesh):
    return jax.shard_map(
        shards,
        mesh=mesh,
        in_specs=(P(("grp", "mic"), None, "row", None), P(), P("grp")),
        out_specs=(P(("grp", "mic"), "row", None, None), P(("grp", "mic"), "row", None, None)),
        check_vma=False,
    )
```

```python
import functools
import math

import jax
import jax.numpy as jnp
import numpy as np
from jax import lax
from jax.experimental import pallas as pl
from jax.experimental.pallas import tpu as pltpu
from jax.sharding import PartitionSpec as P

WCOLS = 128
MESH = pl.DeviceIdType.MESH
BLK = 16
PRODUCT = jnp.float32
MAPS = jnp.bfloat16
PARTS = 4


two_pi = 2.0 * math.pi


def swapped(shard, axis, apart):
    return lax.ppermute(shard, axis, [(i, i ^ 1 << apart) for i in range(lax.axis_size(axis))])


def merged_2(part, axis, combine):
    gathered = jax.tree.map(lambda a: lax.all_gather(a, axis), part)

    def take(source):
        return jax.tree.map(lambda a: lax.dynamic_index_in_dim(a, source, 0, False), gathered)

    return lax.fori_loop(
        1, lax.axis_size(axis), lambda source, state: combine(state, take(source)), take(0)
    )


def phase_table(row_start, row_count, col_start, col_count, period):
    row_ids = row_start + jnp.arange(row_count, dtype=jnp.int32)
    col_ids = col_start + jnp.arange(col_count, dtype=jnp.int32)
    wrapped = row_ids[:, None] * col_ids[None, :] % period
    angles = wrapped.astype(jnp.float32) * (two_pi / period)
    return (jnp.cos(angles), jnp.sin(angles))


def normalize(picture):
    values = picture.astype(jnp.float32)
    centred = values - jnp.mean(values)
    factor = lax.rsqrt(jnp.mean(centred * centred) + 1e-06)
    return (centred * factor).astype(jnp.bfloat16)


def reverse_bits(number, digits):
    result = number * 0
    for digit in range(digits):
        result = result + number // (1 << digit) % 2 * (1 << digits - 1 - digit)
    return result


def combine_maps(first_pair, second_pair):
    return (jnp.maximum(first_pair[0], second_pair[0]), first_pair[1] + second_pair[1])


def shards_general(spectra, bank, orient_index):
    mic_count = spectra.shape[0]
    band_rows = spectra.shape[2]
    length = spectra.shape[3]
    tsize_px = bank.shape[1]
    row_devices = lax.axis_size("row")
    row_place = lax.axis_index("row")
    share_count = orient_index.shape[0] // lax.axis_size("orient")
    chosen = lax.dynamic_slice_in_dim(
        orient_index, lax.axis_index("orient") * share_count, share_count
    )
    templates = jax.vmap(normalize)(bank[chosen])
    cos_y, sin_y = phase_table(row_place * band_rows, band_rows, 0, tsize_px, length)
    left_table = jnp.concatenate([cos_y.astype(jnp.bfloat16), -sin_y.astype(jnp.bfloat16)], 0)
    rowpass = jnp.einsum(
        "ay,oyx->oax", left_table, templates, preferred_element_type=jnp.float32
    ).astype(jnp.bfloat16)
    cos_x, sin_x = phase_table(0, tsize_px, 0, length, length)
    right_table = jnp.concatenate([cos_x.astype(jnp.bfloat16), sin_x.astype(jnp.bfloat16)], 1)
    mixed = jnp.einsum("oax,xk->oak", rowpass, right_table, preferred_element_type=jnp.float32)
    upper_rows = mixed[:, :band_rows]
    lower_rows = mixed[:, band_rows:]
    spec_re = upper_rows[:, :, :length] + lower_rows[:, :, length:]
    spec_im = lower_rows[:, :, :length] - upper_rows[:, :, length:]
    piece = jnp.stack([spec_re, spec_im], 1).astype(jnp.bfloat16)
    cos_e, sin_e = phase_table(0, length, 0, WCOLS, length)
    row_table = jnp.concatenate([cos_e.astype(jnp.bfloat16), sin_e.astype(jnp.bfloat16)], 1)
    updates = []
    for orient_pos in range(share_count):
        tmpl_re = piece[orient_pos, 0].astype(jnp.float32)
        tmpl_im = piece[orient_pos, 1].astype(jnp.float32)
        mic_re = spectra[:, 0].astype(jnp.float32)
        mic_im = spectra[:, 1].astype(jnp.float32)
        prod_re = mic_re * tmpl_re + mic_im * tmpl_im
        prod_im = mic_im * tmpl_re - mic_re * tmpl_im
        product = jnp.stack([prod_re, prod_im], 1).astype(jnp.bfloat16)
        summed = jnp.einsum("mcbk,kw->mcbw", product, row_table, preferred_element_type=jnp.float32)
        part_re = summed[:, 0, :, :WCOLS] - summed[:, 1, :, WCOLS:]
        part_im = summed[:, 0, :, WCOLS:] + summed[:, 1, :, :WCOLS]
        updates.append(jnp.stack([part_re, part_im], 1))
    partial_value = jnp.stack(updates, 1)
    item_total = mic_count * share_count
    values = partial_value.reshape(item_total, 2, band_rows, WCOLS)
    sections = row_devices.bit_length() - 1
    for bit in reversed(range(sections)):
        half_span = 1 << bit
        partner = swapped(values, "row", bit)
        upper_side = row_place // half_span % 2
        offset = row_place % half_span
        twist = offset.astype(jnp.float32) * (math.pi / half_span)
        twist_re = jnp.cos(twist)
        twist_im = jnp.sin(twist)
        differ = partner - values
        rot_re = differ[:, 0] * twist_re - differ[:, 1] * twist_im
        rot_im = differ[:, 0] * twist_im + differ[:, 1] * twist_re
        rotated = jnp.stack([rot_re, rot_im], 1)
        values = jnp.where(upper_side == 1, rotated, values + partner)
    residue = reverse_bits(row_place, sections)
    pixel_rows = residue + row_devices * jnp.arange(band_rows, dtype=jnp.int32)
    local_rows = jnp.arange(band_rows, dtype=jnp.int32)
    wrapped_col = pixel_rows[:, None] * local_rows[None, :] % length
    col_angles = wrapped_col.astype(jnp.float32) * (two_pi / length)
    column_table = jnp.stack([jnp.cos(col_angles), -jnp.sin(col_angles)], 1)
    corr = jnp.einsum("tcj,icjw->itw", column_table, values, precision=lax.Precision.HIGHEST)
    corr = corr * (1.0 / (length * tsize_px))
    corr = corr.reshape(mic_count, share_count, band_rows, WCOLS)
    peak_part = jnp.max(corr, axis=1)
    power_part = jnp.sum(corr * corr, axis=1)
    merged = merged_2((peak_part, power_part), "orient", combine_maps)
    return (merged[0][:, None], merged[1][:, None])


def factors(rows, cols, period, shift=None):
    angle = np.outer(rows, cols) % period * (two_pi / period)
    if shift is not None:
        angle = angle + shift
    return np.stack([np.cos(angle), np.sin(angle)]).astype(np.float32)


def fused_kernel(
    sizes,
    index_ref, spectra_ref, bank_ref, w384, w512, w256, w1024,
    final,
    spec, bank, f384, f512, f256, f1024,
    left, table_x, table_e, col_hi, col_lo, twc, tws, order,
    rows_in, prod, send, recv, v_hi, v_lo, corr_acc, peak, power,
    own, sibling, merged,
    load_sem, send_sem, recv_sem, pair_send, pair_recv,
    map_send, map_recv, fwd_send, fwd_recv,
):
    bands, share, band, length, tsize = sizes
    half = WCOLS // 2
    hb = band // 2
    pb = band // PARTS
    kq = length // 4
    me = lax.axis_index("row")
    core = lax.axis_index("orient")

    loads = [
        pltpu.make_async_copy(source, target, load_sem.at[n])
        for n, (source, target) in enumerate(
            [(w384, f384), (w512, f512), (w256, f256), (w1024, f1024), (bank_ref, bank), (spectra_ref, spec)]
        )
    ]
    for load in loads:
        load.start()
    barrier = pltpu.get_barrier_semaphore()
    for k in range(1, bands):
        pl.semaphore_signal(
            barrier, inc=1, device_id={"row": lax.rem(me + k, bands)}, device_id_type=MESH
        )
    pl.semaphore_signal(barrier, inc=1, device_id={"orient": 1 - core}, device_id_type=MESH)

    def rows_of(block):
        return pl.ds(pl.multiple_of(block * BLK, BLK), BLK)

    at = lax.broadcasted_iota(jnp.int32, (tsize, 4 * WCOLS), 1)
    x = lax.broadcasted_iota(jnp.int32, (tsize, 4 * WCOLS), 0)
    picked = (x == 4 * (at % WCOLS) + at // WCOLS) & (at % WCOLS < tsize // 4)
    order[...] = jnp.where(picked, 1.0, 0.0).astype(jnp.bfloat16)

    loads[0].wait()
    n_left = length // BLK

    def left_body(group, carry):
        cb, sb = f384[0, pl.ds(n_left, BLK), :], f384[1, pl.ds(n_left, BLK), :]
        for block in range(8):
            a = group * 8 + block
            row = me * (band // BLK) + a
            ca, sa = f384[0, pl.ds(row, 1), :], f384[1, pl.ds(row, 1), :]
            left[0, rows_of(a), :] = (ca * cb - sa * sb).astype(jnp.bfloat16)
            left[1, rows_of(a), :] = (-(sa * cb + ca * sb)).astype(jnp.bfloat16)
        return carry

    lax.fori_loop(0, band // BLK // 8, left_body, 0)
    loads[1].wait()

    def tx_body(a, carry):
        ca, sa = f512[0, pl.ds(a, 1), :], f512[1, pl.ds(a, 1), :]
        for s in range(4):
            where = pl.ds((s + 1) * BLK, BLK)
            cb, sb = f512[0, where, :], f512[1, where, :]
            table_x[s, rows_of(a), :] = (ca * cb - sa * sb).astype(jnp.bfloat16)
            table_x[s, rows_of(a + WCOLS // BLK), :] = (sa * cb + ca * sb).astype(jnp.bfloat16)
        return carry

    lax.fori_loop(0, WCOLS // BLK, tx_body, 0)
    loads[2].wait()
    ft = kq // 2

    def te_body(group, carry):
        per = ft // BLK
        tile, u = group % 2, group // 2
        cb = [f256[0, pl.ds(n_left + part * BLK, BLK), :] for part in range(2)]
        sb = [f256[1, pl.ds(n_left + part * BLK, BLK), :] for part in range(2)]
        for block in range(per):
            a = group * per + block
            ca, sa = f256[0, pl.ds(a, 1), :], f256[1, pl.ds(a, 1), :]
            for part in range(2):
                row = (part * 4 + u) * ft + block * BLK
                table_e[tile, pl.ds(pl.multiple_of(row, BLK), BLK), :] = (
                    ca * cb[part] - sa * sb[part]
                ).astype(jnp.bfloat16)
        return carry

    lax.fori_loop(0, 8, te_body, 0)
    pl.semaphore_wait(barrier, bands)
    loads[4].wait()

    def orient_body(o, carry):
        picture = bank[index_ref[core * share + o]].astype(jnp.float32)
        centred = picture - jnp.mean(picture)
        scale = lax.rsqrt(jnp.mean(centred * centred) + 1e-06)
        template = (centred * scale).astype(jnp.bfloat16)
        template = jnp.dot(template, order[...], preferred_element_type=jnp.float32)
        template = template.astype(jnp.bfloat16)
        for n in range(2):
            value = jnp.dot(left[n], template, preferred_element_type=jnp.float32)
            value = value.astype(jnp.bfloat16)
            for s in range(4):
                piece = value[:, s * WCOLS : (s + 1) * WCOLS]
                if n == 0:
                    rows_in[s, 0, :, pl.ds(0, WCOLS)] = piece
                    rows_in[s, 1, :, pl.ds(WCOLS, WCOLS)] = -piece
                else:
                    rows_in[s, 0, :, pl.ds(WCOLS, WCOLS)] = piece
                    rows_in[s, 1, :, pl.ds(0, WCOLS)] = piece

        @pl.when(o == 0)
        def _():
            loads[5].wait()

        def part_body(h, inner):
            rows = pl.ds(pl.multiple_of(h * pb, pb), pb)
            total = None
            for tile in range(2):
                cols = pl.ds(tile * ft, ft)
                re, im = [], []
                for s in range(4):
                    wide = table_x[s, :, cols]
                    re.append(jnp.dot(rows_in[s, 0, rows, :], wide, preferred_element_type=jnp.float32))
                    im.append(jnp.dot(rows_in[s, 1, rows, :], wide, preferred_element_type=jnp.float32))
                s02r, d02r, s13r, d13r = re[0] + re[2], re[0] - re[2], re[1] + re[3], re[1] - re[3]
                s02i, d02i, s13i, d13i = im[0] + im[2], im[0] - im[2], im[1] + im[3], im[1] - im[3]
                quads = [
                    (s02r + s13r, s02i + s13i),
                    (d02r + d13i, d02i - d13r),
                    (s02r - s13r, s02i - s13i),
                    (d02r - d13i, d02i + d13r),
                ]
                for u, (t_re, t_im) in enumerate(quads):
                    t_re = t_re.astype(jnp.bfloat16).astype(PRODUCT)
                    t_im = t_im.astype(jnp.bfloat16).astype(PRODUCT)
                    where = pl.ds(u * kq + tile * ft, ft)
                    for m in range(2):
                        m_re = spec[m, 0, rows, where].astype(PRODUCT)
                        m_im = spec[m, 1, rows, where].astype(PRODUCT)
                        p_re = (m_re * t_re + m_im * t_im).astype(jnp.bfloat16)
                        p_im = (m_im * t_re - m_re * t_im).astype(jnp.bfloat16)
                        prod[tile, pl.ds(m * pb, pb), pl.ds(u * ft, ft)] = p_re
                        prod[tile, pl.ds(m * pb, pb), pl.ds((4 + u) * ft, ft)] = p_im
                value = jnp.dot(prod[tile], table_e[tile], preferred_element_type=jnp.float32)
                total = value if total is None else total + value
            total = total.astype(jnp.bfloat16)
            for d in range(bands):
                m, xh = d // 2, d % 2
                tile = total[m * pb : (m + 1) * pb, xh * WCOLS : (xh + 1) * WCOLS]

                @pl.when(me == d)
                def _():
                    recv[me, o, rows, :] = tile

                @pl.when(me != d)
                def _():
                    send[d, o, rows, :] = tile

            for k in (2, 1, 3):
                part_copy(k, lax.rem(me + k, bands), me, o, h).start()
            return inner

        lax.fori_loop(0, PARTS, part_body, 0)
        return carry

    def part_copy(k, dest, source, o, h):
        rows = pl.ds(pl.multiple_of(h * pb, pb), pb)
        return pltpu.make_async_remote_copy(
            src_ref=send.at[dest, o, rows, :], dst_ref=recv.at[source, o, rows, :],
            send_sem=send_sem.at[k, o, h], recv_sem=recv_sem.at[source, o, h],
            device_id={"row": dest}, device_id_type=MESH,
        )

    lax.fori_loop(0, share, orient_body, 0)
    loads[3].wait()
    n_col = band // BLK

    def col_body(a, carry):
        ca, sa = f1024[0, pl.ds(a, 1), :], f1024[1, pl.ds(a, 1), :]
        value = ca * f1024[0, pl.ds(n_col, BLK), :] - sa * f1024[1, pl.ds(n_col, BLK), :]
        high = value.astype(jnp.bfloat16)
        col_hi[rows_of(a), :] = high
        col_lo[rows_of(a), :] = (value - high.astype(jnp.float32)).astype(jnp.bfloat16)
        base = n_left + BLK
        ta, ua = f384[0, pl.ds(base + a, 1), :], f384[1, pl.ds(base + a, 1), :]
        where = pl.ds(base + n_col, BLK)
        tb, ub = f384[0, where, :], f384[1, where, :]
        lane = lax.broadcasted_iota(jnp.int32, (BLK, 3 * WCOLS), 1) % WCOLS
        twc[rows_of(a), :] = ta * tb - ua * ub
        sine = ua * tb + ta * ub
        tws[rows_of(a), :] = jnp.where(lane < half, -sine, sine)
        return carry

    lax.fori_loop(0, band // BLK, col_body, 0)

    peak[...] = jnp.full_like(peak, -1e30)
    power[...] = jnp.zeros_like(power)
    factor = 1.0 / (length * tsize)
    rc = 64

    def column_body(o, carry):
        corr_acc[...] = jnp.zeros_like(corr_acc)

        def part_column(h, inner):
            for k in range(1, bands):
                source = lax.rem(me + k, bands)
                part_copy(k, source, source, o, h).wait_recv()
            for c in range(pb // rc):
                rows = pl.ds(pl.multiple_of(h * pb + c * rc, rc), rc)
                lane = lax.broadcasted_iota(jnp.int32, (rc, WCOLS), 1)
                first = lane < half
                b0, b1, b2, b3 = [recv[b, o, rows, :].astype(jnp.float32) for b in range(4)]
                s02, d02, s13, d13 = b0 + b2, b0 - b2, b1 + b3, b1 - b3
                turned = pltpu.roll(d13, half, 1)
                turned = jnp.where(first, -turned, turned)
                u = [s02 + s13, d02 + turned, s02 - s13, d02 - turned]
                v = [u[0]]
                for rho in range(1, 4):
                    span = pl.ds((rho - 1) * WCOLS, WCOLS)
                    v.append(
                        u[rho] * twc[rows, span] + pltpu.roll(u[rho], half, 1) * tws[rows, span]
                    )
                for pair in range(2):
                    even, odd = v[2 * pair], v[2 * pair + 1]
                    v_re = jnp.where(first, even, pltpu.roll(odd, half, 1))
                    v_im = jnp.where(first, pltpu.roll(even, half, 1), odd)
                    span = pl.ds(pair * WCOLS, WCOLS)
                    for part, value in enumerate((v_re, v_im)):
                        high = value.astype(jnp.bfloat16)
                        where = pl.ds(part * pb + c * rc, rc)
                        v_hi[where, span] = high
                        v_lo[where, span] = (value - high.astype(jnp.float32)).astype(jnp.bfloat16)
            cols = pl.ds(pl.multiple_of(h * 2 * pb, 2 * pb), 2 * pb)
            high, low = col_hi[:, cols], col_lo[:, cols]
            corr = jnp.dot(high, v_hi[...], preferred_element_type=jnp.float32)
            corr += jnp.dot(low, v_hi[...], preferred_element_type=jnp.float32)
            corr += jnp.dot(high, v_lo[...], preferred_element_type=jnp.float32)
            corr_acc[...] += corr
            return inner

        lax.fori_loop(0, PARTS, part_column, 0)
        corr = corr_acc[...] * factor
        peak[...] = jnp.maximum(peak[...], corr)
        power[...] += corr * corr
        return carry

    lax.fori_loop(0, share, column_body, 0)

    first = lax.broadcasted_iota(jnp.int32, (band, WCOLS), 1) < half
    for q in range(4):
        rho = (q % 2) * 2 + q // 2
        span = pl.ds(rho // 2 * WCOLS, WCOLS)
        hi, po = peak[:, span], power[:, span]
        if rho % 2 == 0:
            own[q] = jnp.where(first, hi, pltpu.roll(po, half, 1))
        else:
            own[q] = jnp.where(first, pltpu.roll(hi, half, 1), po)

    mine = pl.ds(pl.multiple_of(core * hb, hb), hb)
    theirs = pl.ds(pl.multiple_of((1 - core) * hb, hb), hb)
    def swap(k):
        q = lax.rem(me + k, bands)
        return pltpu.make_async_remote_copy(
            src_ref=own.at[q, theirs, :], dst_ref=sibling.at[q],
            send_sem=pair_send.at[k], recv_sem=pair_recv.at[k],
            device_id={"orient": 1 - core}, device_id_type=MESH,
        )

    for k in (2, 1, 3, 0):
        swap(k).start()
    first = lax.broadcasted_iota(jnp.int32, (hb, WCOLS), 1) < half

    def map_copy(k, source):
        dest = lax.rem(me + k, bands)
        return pltpu.make_async_remote_copy(
            src_ref=merged.at[dest], dst_ref=final.at[source, mine, :],
            send_sem=map_send.at[k], recv_sem=map_recv.at[source],
            device_id={"row": dest}, device_id_type=MESH,
        )

    def forward(source, rows):
        return pltpu.make_async_remote_copy(
            src_ref=final.at[source, rows, :], dst_ref=final.at[source, rows, :],
            send_sem=fwd_send.at[source], recv_sem=fwd_recv.at[source],
            device_id={"orient": 1 - core}, device_id_type=MESH,
        )

    for k in (2, 1, 3, 0):
        swap(k).wait_recv()
        q = lax.rem(me + k, bands)
        one, two = own[q, mine, :], sibling[q]
        total = jnp.where(first, jnp.maximum(one, two), one + two).astype(final.dtype)
        if k == 0:
            final[me, mine, :] = total
        else:
            merged[q] = total
            map_copy(k, me).start()
    forward(me, mine).start()
    for k in (1, 3, 2):
        source = lax.rem(me + k, bands)
        map_copy(k, source).wait_recv()
        forward(source, mine).start()
    for source in range(4):
        forward(source, theirs).wait_recv()
    for source in range(4):
        forward(source, mine).wait_send()
    for k in range(1, bands):
        map_copy(k, me).wait_send()
    for k in range(bands):
        swap(k).wait_send()

    def drain(o, carry):
        for k in range(1, bands):
            dest = lax.rem(me + k, bands)
            for h in range(PARTS):
                part_copy(k, dest, me, o, h).wait_send()
        return carry

    lax.fori_loop(0, share, drain, 0)


def assemble_kernel(maps, peak_ref, power_ref):
    half = WCOLS // 2
    first = lax.broadcasted_iota(jnp.int32, maps.shape[1:], 1) < half
    for m in range(2):
        a, b = maps[2 * m].astype(jnp.float32), maps[2 * m + 1].astype(jnp.float32)
        peak_ref[m, 0] = jnp.where(first, a, pltpu.roll(b, half, 1))
        power_ref[m, 0] = jnp.where(first, pltpu.roll(a, half, 1), b)


def shards_fused(spectra, bank, orient_index):
    band = spectra.shape[2]
    length = spectra.shape[3]
    tsize = bank.shape[1]
    bands = lax.axis_size("row")
    share = orient_index.shape[0] // lax.axis_size("orient")
    half = WCOLS // 2
    bf, f32 = jnp.bfloat16, jnp.float32

    small = np.arange(BLK)
    y = np.arange(tsize)
    kq = np.arange(length // 4)
    lane = np.arange(2 * WCOLS)
    lane_x = lane // WCOLS * half + lane % half
    is_im = lane % WCOLS >= half
    quarter = two_pi / 4
    steps = np.arange(length // BLK) * BLK
    short = np.arange(band // BLK) * BLK
    pb = band // PARTS
    at = np.arange(2 * band)
    col_j = at // (2 * pb) * pb + at % pb
    col_shift = np.where(at // pb % 2 == 0, 0.0, quarter)
    rho = np.repeat(np.arange(1, 4), WCOLS)
    spread = np.concatenate([np.arange(BLK) * 4 * BLK] + [4 * small + s for s in range(4)])
    w384 = np.concatenate(
        [
            factors(steps, y, length),
            factors(small, y, length),
            factors(short, rho, length),
            factors(small, rho, length),
        ],
        1,
    )
    w512 = factors(spread, kq, length)
    w256 = np.concatenate(
        [
            factors(steps, lane_x, length),
            factors(small, lane_x, length, np.where(is_im, -quarter, 0.0)),
            factors(small, lane_x, length, np.where(is_im, 0.0, quarter)),
        ],
        1,
    )
    w1024 = np.concatenate(
        [factors(short, col_j, band), factors(small, col_j, band, col_shift)], 1
    )
    tables = [w384, w512, w256, w1024]
    vmem = pl.BlockSpec(memory_space=pltpu.VMEM)
    hbm = pl.BlockSpec(memory_space=pl.ANY)
    dma = pltpu.SemaphoreType.DMA
    maps = pl.pallas_call(
        functools.partial(fused_kernel, (bands, share, band, length, tsize)),
        out_shape=jax.ShapeDtypeStruct((4, band, WCOLS), MAPS),
        in_specs=[pl.BlockSpec(memory_space=pltpu.SMEM)] + [hbm] * (2 + len(tables)),
        out_specs=vmem,
        scratch_shapes=[
            pltpu.VMEM(spectra.shape, bf),
            pltpu.VMEM(bank.shape, bf),
        ]
        + [pltpu.VMEM(table.shape, f32) for table in tables]
        + [
            pltpu.VMEM((2, band, tsize), bf),
            pltpu.VMEM((4, 2 * WCOLS, length // 4), bf),
            pltpu.VMEM((2, length, 2 * WCOLS), bf),
            pltpu.VMEM((band, 2 * band), bf),
            pltpu.VMEM((band, 2 * band), bf),
            pltpu.VMEM((band, 3 * WCOLS), f32),
            pltpu.VMEM((band, 3 * WCOLS), f32),
            pltpu.VMEM((tsize, 4 * WCOLS), bf),
            pltpu.VMEM((4, 2, band, 2 * WCOLS), bf),
            pltpu.VMEM((2, 2 * band // PARTS, length), bf),
            pltpu.VMEM((bands, share, band, WCOLS), bf),
            pltpu.VMEM((bands, share, band, WCOLS), bf),
            pltpu.VMEM((2 * band // PARTS, 2 * WCOLS), bf),
            pltpu.VMEM((2 * band // PARTS, 2 * WCOLS), bf),
            pltpu.VMEM((band, 2 * WCOLS), f32),
            pltpu.VMEM((band, 2 * WCOLS), f32),
            pltpu.VMEM((band, 2 * WCOLS), f32),
            pltpu.VMEM((4, band, WCOLS), f32),
            pltpu.VMEM((4, band // 2, WCOLS), f32),
            pltpu.VMEM((4, band // 2, WCOLS), MAPS),
            dma((6,)),
            dma((bands, share, PARTS)),
            dma((bands, share, PARTS)),
            dma((bands,)),
            dma((bands,)),
            dma((bands,)),
            dma((bands,)),
            dma((bands,)),
            dma((bands,)),
        ],
        compiler_params=pltpu.CompilerParams(
            collective_id=0, has_side_effects=True, vmem_limit_bytes=58 << 20
        ),
    )(orient_index, spectra, bank, *tables)
    out = jax.ShapeDtypeStruct((2, 1, band, WCOLS), f32)
    return pl.pallas_call(
        assemble_kernel, out_shape=(out, out), in_specs=[vmem], out_specs=(vmem, vmem)
    )(maps)


def shards(spectra, bank, orient_index):
    fits = (
        lax.axis_size("row") == 4
        and lax.axis_size("orient") == 2
        and spectra.shape[0] == 2
        and spectra.shape[2] % 128 == 0
        and bank.shape[1] == 3 * WCOLS
        and spectra.shape[3] == 4 * spectra.shape[2]
    )
    body = shards_fused if fits else shards_general
    return body(spectra, bank, orient_index)


def solution(mesh):
    return jax.shard_map(
        shards,
        mesh=mesh,
        in_specs=(P(("grp", "mic"), None, "row", None), P(), P("grp")),
        out_specs=(P(("grp", "mic"), "row", None, None), P(("grp", "mic"), "row", None, None)),
        check_vma=False,
    )
```

```python
import functools
import math

import jax
import jax.numpy as jnp
import numpy as np
from jax import lax
from jax.experimental import pallas as pl
from jax.experimental.pallas import tpu as pltpu
from jax.sharding import PartitionSpec as P

WCOLS = 128
MESH = pl.DeviceIdType.MESH
BLK = 16
PRODUCT = jnp.float32
MAPS = jnp.bfloat16
PARTS = 4


two_pi = 2.0 * math.pi


def swapped(shard, axis, apart):
    return lax.ppermute(shard, axis, [(i, i ^ 1 << apart) for i in range(lax.axis_size(axis))])


def merged_2(part, axis, combine):
    gathered = jax.tree.map(lambda a: lax.all_gather(a, axis), part)

    def take(source):
        return jax.tree.map(lambda a: lax.dynamic_index_in_dim(a, source, 0, False), gathered)

    return lax.fori_loop(
        1, lax.axis_size(axis), lambda source, state: combine(state, take(source)), take(0)
    )


def phase_table(row_start, row_count, col_start, col_count, period):
    row_ids = row_start + jnp.arange(row_count, dtype=jnp.int32)
    col_ids = col_start + jnp.arange(col_count, dtype=jnp.int32)
    wrapped = row_ids[:, None] * col_ids[None, :] % period
    angles = wrapped.astype(jnp.float32) * (two_pi / period)
    return (jnp.cos(angles), jnp.sin(angles))


def normalize(picture):
    values = picture.astype(jnp.float32)
    centred = values - jnp.mean(values)
    factor = lax.rsqrt(jnp.mean(centred * centred) + 1e-06)
    return (centred * factor).astype(jnp.bfloat16)


def reverse_bits(number, digits):
    result = number * 0
    for digit in range(digits):
        result = result + number // (1 << digit) % 2 * (1 << digits - 1 - digit)
    return result


def combine_maps(first_pair, second_pair):
    return (jnp.maximum(first_pair[0], second_pair[0]), first_pair[1] + second_pair[1])


def shards_general(spectra, bank, orient_index):
    mic_count = spectra.shape[0]
    band_rows = spectra.shape[2]
    length = spectra.shape[3]
    tsize_px = bank.shape[1]
    row_devices = lax.axis_size("row")
    row_place = lax.axis_index("row")
    share_count = orient_index.shape[0] // lax.axis_size("orient")
    chosen = lax.dynamic_slice_in_dim(
        orient_index, lax.axis_index("orient") * share_count, share_count
    )
    templates = jax.vmap(normalize)(bank[chosen])
    cos_y, sin_y = phase_table(row_place * band_rows, band_rows, 0, tsize_px, length)
    left_table = jnp.concatenate([cos_y.astype(jnp.bfloat16), -sin_y.astype(jnp.bfloat16)], 0)
    rowpass = jnp.einsum(
        "ay,oyx->oax", left_table, templates, preferred_element_type=jnp.float32
    ).astype(jnp.bfloat16)
    cos_x, sin_x = phase_table(0, tsize_px, 0, length, length)
    right_table = jnp.concatenate([cos_x.astype(jnp.bfloat16), sin_x.astype(jnp.bfloat16)], 1)
    mixed = jnp.einsum("oax,xk->oak", rowpass, right_table, preferred_element_type=jnp.float32)
    upper_rows = mixed[:, :band_rows]
    lower_rows = mixed[:, band_rows:]
    spec_re = upper_rows[:, :, :length] + lower_rows[:, :, length:]
    spec_im = lower_rows[:, :, :length] - upper_rows[:, :, length:]
    piece = jnp.stack([spec_re, spec_im], 1).astype(jnp.bfloat16)
    cos_e, sin_e = phase_table(0, length, 0, WCOLS, length)
    row_table = jnp.concatenate([cos_e.astype(jnp.bfloat16), sin_e.astype(jnp.bfloat16)], 1)
    updates = []
    for orient_pos in range(share_count):
        tmpl_re = piece[orient_pos, 0].astype(jnp.float32)
        tmpl_im = piece[orient_pos, 1].astype(jnp.float32)
        mic_re = spectra[:, 0].astype(jnp.float32)
        mic_im = spectra[:, 1].astype(jnp.float32)
        prod_re = mic_re * tmpl_re + mic_im * tmpl_im
        prod_im = mic_im * tmpl_re - mic_re * tmpl_im
        product = jnp.stack([prod_re, prod_im], 1).astype(jnp.bfloat16)
        summed = jnp.einsum("mcbk,kw->mcbw", product, row_table, preferred_element_type=jnp.float32)
        part_re = summed[:, 0, :, :WCOLS] - summed[:, 1, :, WCOLS:]
        part_im = summed[:, 0, :, WCOLS:] + summed[:, 1, :, :WCOLS]
        updates.append(jnp.stack([part_re, part_im], 1))
    partial_value = jnp.stack(updates, 1)
    item_total = mic_count * share_count
    values = partial_value.reshape(item_total, 2, band_rows, WCOLS)
    sections = row_devices.bit_length() - 1
    for bit in reversed(range(sections)):
        half_span = 1 << bit
        partner = swapped(values, "row", bit)
        upper_side = row_place // half_span % 2
        offset = row_place % half_span
        twist = offset.astype(jnp.float32) * (math.pi / half_span)
        twist_re = jnp.cos(twist)
        twist_im = jnp.sin(twist)
        differ = partner - values
        rot_re = differ[:, 0] * twist_re - differ[:, 1] * twist_im
        rot_im = differ[:, 0] * twist_im + differ[:, 1] * twist_re
        rotated = jnp.stack([rot_re, rot_im], 1)
        values = jnp.where(upper_side == 1, rotated, values + partner)
    residue = reverse_bits(row_place, sections)
    pixel_rows = residue + row_devices * jnp.arange(band_rows, dtype=jnp.int32)
    local_rows = jnp.arange(band_rows, dtype=jnp.int32)
    wrapped_col = pixel_rows[:, None] * local_rows[None, :] % length
    col_angles = wrapped_col.astype(jnp.float32) * (two_pi / length)
    column_table = jnp.stack([jnp.cos(col_angles), -jnp.sin(col_angles)], 1)
    corr = jnp.einsum("tcj,icjw->itw", column_table, values, precision=lax.Precision.HIGHEST)
    corr = corr * (1.0 / (length * tsize_px))
    corr = corr.reshape(mic_count, share_count, band_rows, WCOLS)
    peak_part = jnp.max(corr, axis=1)
    power_part = jnp.sum(corr * corr, axis=1)
    merged = merged_2((peak_part, power_part), "orient", combine_maps)
    return (merged[0][:, None], merged[1][:, None])


def factors(rows, cols, period, shift=None):
    angle = np.outer(rows, cols) % period * (two_pi / period)
    if shift is not None:
        angle = angle + shift
    return np.stack([np.cos(angle), np.sin(angle)]).astype(np.float32)


def fused_kernel(
    sizes,
    index_ref, spectra_ref, bank_ref, w384, w512, w256, w1024,
    final,
    spec, bank, f384, f512, f256, f1024,
    left, table_x, table_e, col_hi, col_lo, twc, tws, order,
    rows_in, prod, send, recv, v_hi, v_lo, corr_acc, peak, power,
    own, sibling, merged,
    load_sem, send_sem, recv_sem, pair_send, pair_recv,
    map_send, map_recv, fwd_send, fwd_recv,
):
    bands, share, band, length, tsize = sizes
    half = WCOLS // 2
    hb = band // 2
    pb = band // PARTS
    kq = length // 4
    me = lax.axis_index("row")
    core = lax.axis_index("orient")

    loads = [
        pltpu.make_async_copy(source, target, load_sem.at[n])
        for n, (source, target) in enumerate(
            [(w384, f384), (w512, f512), (w256, f256), (w1024, f1024), (bank_ref, bank), (spectra_ref, spec)]
        )
    ]
    for load in loads:
        load.start()
    barrier = pltpu.get_barrier_semaphore()
    for k in range(1, bands):
        pl.semaphore_signal(
            barrier, inc=1, device_id={"row": lax.rem(me + k, bands)}, device_id_type=MESH
        )
    pl.semaphore_signal(barrier, inc=1, device_id={"orient": 1 - core}, device_id_type=MESH)

    def rows_of(block):
        return pl.ds(pl.multiple_of(block * BLK, BLK), BLK)

    at = lax.broadcasted_iota(jnp.int32, (tsize, 4 * WCOLS), 1)
    x = lax.broadcasted_iota(jnp.int32, (tsize, 4 * WCOLS), 0)
    picked = (x == 4 * (at % WCOLS) + at // WCOLS) & (at % WCOLS < tsize // 4)
    order[...] = jnp.where(picked, 1.0, 0.0).astype(jnp.bfloat16)

    loads[0].wait()
    n_left = length // BLK

    def left_body(group, carry):
        cb, sb = f384[0, pl.ds(n_left, BLK), :], f384[1, pl.ds(n_left, BLK), :]
        for block in range(8):
            a = group * 8 + block
            row = me * (band // BLK) + a
            ca, sa = f384[0, pl.ds(row, 1), :], f384[1, pl.ds(row, 1), :]
            left[0, rows_of(a), :] = (ca * cb - sa * sb).astype(jnp.bfloat16)
            left[1, rows_of(a), :] = (-(sa * cb + ca * sb)).astype(jnp.bfloat16)
        return carry

    lax.fori_loop(0, band // BLK // 8, left_body, 0)
    loads[1].wait()

    def tx_body(a, carry):
        ca, sa = f512[0, pl.ds(a, 1), :], f512[1, pl.ds(a, 1), :]
        for s in range(4):
            where = pl.ds((s + 1) * BLK, BLK)
            cb, sb = f512[0, where, :], f512[1, where, :]
            table_x[s, rows_of(a), :] = (ca * cb - sa * sb).astype(jnp.bfloat16)
            table_x[s, rows_of(a + WCOLS // BLK), :] = (sa * cb + ca * sb).astype(jnp.bfloat16)
        return carry

    lax.fori_loop(0, WCOLS // BLK, tx_body, 0)
    loads[2].wait()
    ft = kq // 2

    def te_body(group, carry):
        per = ft // BLK
        tile, u = group % 2, group // 2
        cb = [f256[0, pl.ds(n_left + part * BLK, BLK), :] for part in range(2)]
        sb = [f256[1, pl.ds(n_left + part * BLK, BLK), :] for part in range(2)]
        for block in range(per):
            a = group * per + block
            ca, sa = f256[0, pl.ds(a, 1), :], f256[1, pl.ds(a, 1), :]
            for part in range(2):
                row = (part * 4 + u) * ft + block * BLK
                table_e[tile, pl.ds(pl.multiple_of(row, BLK), BLK), :] = (
                    ca * cb[part] - sa * sb[part]
                ).astype(jnp.bfloat16)
        return carry

    lax.fori_loop(0, 8, te_body, 0)
    pl.semaphore_wait(barrier, bands)
    loads[4].wait()

    def orient_body(o, carry):
        picture = bank[index_ref[core * share + o]].astype(jnp.float32)
        centred = picture - jnp.mean(picture)
        scale = lax.rsqrt(jnp.mean(centred * centred) + 1e-06)
        template = (centred * scale).astype(jnp.bfloat16)
        template = jnp.dot(template, order[...], preferred_element_type=jnp.float32)
        template = template.astype(jnp.bfloat16)
        for n in range(2):
            value = jnp.dot(left[n], template, preferred_element_type=jnp.float32)
            value = value.astype(jnp.bfloat16)
            for s in range(4):
                piece = value[:, s * WCOLS : (s + 1) * WCOLS]
                if n == 0:
                    rows_in[s, 0, :, pl.ds(0, WCOLS)] = piece
                    rows_in[s, 1, :, pl.ds(WCOLS, WCOLS)] = -piece
                else:
                    rows_in[s, 0, :, pl.ds(WCOLS, WCOLS)] = piece
                    rows_in[s, 1, :, pl.ds(0, WCOLS)] = piece

        @pl.when(o == 0)
        def _():
            loads[5].wait()

        def part_body(h, inner):
            rows = pl.ds(pl.multiple_of(h * pb, pb), pb)
            total = None
            for tile in range(2):
                cols = pl.ds(tile * ft, ft)
                re, im = [], []
                for s in range(4):
                    wide = table_x[s, :, cols]
                    re.append(jnp.dot(rows_in[s, 0, rows, :], wide, preferred_element_type=jnp.float32))
                    im.append(jnp.dot(rows_in[s, 1, rows, :], wide, preferred_element_type=jnp.float32))
                s02r, d02r, s13r, d13r = re[0] + re[2], re[0] - re[2], re[1] + re[3], re[1] - re[3]
                s02i, d02i, s13i, d13i = im[0] + im[2], im[0] - im[2], im[1] + im[3], im[1] - im[3]
                quads = [
                    (s02r + s13r, s02i + s13i),
                    (d02r + d13i, d02i - d13r),
                    (s02r - s13r, s02i - s13i),
                    (d02r - d13i, d02i + d13r),
                ]
                for u, (t_re, t_im) in enumerate(quads):
                    t_re = t_re.astype(jnp.bfloat16).astype(PRODUCT)
                    t_im = t_im.astype(jnp.bfloat16).astype(PRODUCT)
                    where = pl.ds(u * kq + tile * ft, ft)
                    for m in range(2):
                        m_re = spec[m, 0, rows, where].astype(PRODUCT)
                        m_im = spec[m, 1, rows, where].astype(PRODUCT)
                        p_re = (m_re * t_re + m_im * t_im).astype(jnp.bfloat16)
                        p_im = (m_im * t_re - m_re * t_im).astype(jnp.bfloat16)
                        prod[tile, pl.ds(m * pb, pb), pl.ds(u * ft, ft)] = p_re
                        prod[tile, pl.ds(m * pb, pb), pl.ds((4 + u) * ft, ft)] = p_im
                value = jnp.dot(prod[tile], table_e[tile], preferred_element_type=jnp.float32)
                total = value if total is None else total + value
            total = total.astype(jnp.bfloat16)
            for d in range(bands):
                m, xh = d // 2, d % 2
                tile = total[m * pb : (m + 1) * pb, xh * WCOLS : (xh + 1) * WCOLS]

                @pl.when(me == d)
                def _():
                    recv[me, o, rows, :] = tile

                @pl.when(me != d)
                def _():
                    send[d, o, rows, :] = tile

            for k in (2, 1, 3):
                part_copy(k, lax.rem(me + k, bands), me, o, h).start()
            return inner

        lax.fori_loop(0, PARTS, part_body, 0)
        return carry

    def part_copy(k, dest, source, o, h):
        rows = pl.ds(pl.multiple_of(h * pb, pb), pb)
        return pltpu.make_async_remote_copy(
            src_ref=send.at[dest, o, rows, :], dst_ref=recv.at[source, o, rows, :],
            send_sem=send_sem.at[k, o, h], recv_sem=recv_sem.at[source, o, h],
            device_id={"row": dest}, device_id_type=MESH,
        )

    lax.fori_loop(0, share, orient_body, 0)
    loads[3].wait()
    n_col = band // BLK

    def col_body(a, carry):
        ca, sa = f1024[0, pl.ds(a, 1), :], f1024[1, pl.ds(a, 1), :]
        value = ca * f1024[0, pl.ds(n_col, BLK), :] - sa * f1024[1, pl.ds(n_col, BLK), :]
        high = value.astype(jnp.bfloat16)
        col_hi[rows_of(a), :] = high
        col_lo[rows_of(a), :] = (value - high.astype(jnp.float32)).astype(jnp.bfloat16)
        base = n_left + BLK
        ta, ua = f384[0, pl.ds(base + a, 1), :], f384[1, pl.ds(base + a, 1), :]
        where = pl.ds(base + n_col, BLK)
        tb, ub = f384[0, where, :], f384[1, where, :]
        lane = lax.broadcasted_iota(jnp.int32, (BLK, 3 * WCOLS), 1) % WCOLS
        twc[rows_of(a), :] = ta * tb - ua * ub
        sine = ua * tb + ta * ub
        tws[rows_of(a), :] = jnp.where(lane < half, -sine, sine)
        return carry

    lax.fori_loop(0, band // BLK, col_body, 0)

    peak[...] = jnp.full_like(peak, -1e30)
    power[...] = jnp.zeros_like(power)
    factor = 1.0 / (length * tsize)
    rc = 64

    def column_body(o, carry):
        corr_acc[...] = jnp.zeros_like(corr_acc)

        def part_column(h, inner):
            for k in range(1, bands):
                source = lax.rem(me + k, bands)
                part_copy(k, source, source, o, h).wait_recv()
            for c in range(pb // rc):
                rows = pl.ds(pl.multiple_of(h * pb + c * rc, rc), rc)
                lane = lax.broadcasted_iota(jnp.int32, (rc, WCOLS), 1)
                first = lane < half
                b0, b1, b2, b3 = [recv[b, o, rows, :].astype(jnp.float32) for b in range(4)]
                s02, d02, s13, d13 = b0 + b2, b0 - b2, b1 + b3, b1 - b3
                turned = pltpu.roll(d13, half, 1)
                turned = jnp.where(first, -turned, turned)
                u = [s02 + s13, d02 + turned, s02 - s13, d02 - turned]
                v = [u[0]]
                for rho in range(1, 4):
                    span = pl.ds((rho - 1) * WCOLS, WCOLS)
                    v.append(
                        u[rho] * twc[rows, span] + pltpu.roll(u[rho], half, 1) * tws[rows, span]
                    )
                for pair in range(2):
                    even, odd = v[2 * pair], v[2 * pair + 1]
                    v_re = jnp.where(first, even, pltpu.roll(odd, half, 1))
                    v_im = jnp.where(first, pltpu.roll(even, half, 1), odd)
                    span = pl.ds(pair * WCOLS, WCOLS)
                    for part, value in enumerate((v_re, v_im)):
                        high = value.astype(jnp.bfloat16)
                        where = pl.ds(part * pb + c * rc, rc)
                        v_hi[where, span] = high
                        v_lo[where, span] = (value - high.astype(jnp.float32)).astype(jnp.bfloat16)
            cols = pl.ds(pl.multiple_of(h * 2 * pb, 2 * pb), 2 * pb)
            high, low = col_hi[:, cols], col_lo[:, cols]
            corr = jnp.dot(high, v_hi[...], preferred_element_type=jnp.float32)
            corr += jnp.dot(low, v_hi[...], preferred_element_type=jnp.float32)
            corr += jnp.dot(high, v_lo[...], preferred_element_type=jnp.float32)
            corr_acc[...] += corr
            return inner

        lax.fori_loop(0, PARTS, part_column, 0)
        corr = corr_acc[...] * factor
        peak[...] = jnp.maximum(peak[...], corr)
        power[...] += corr * corr
        return carry

    lax.fori_loop(0, share, column_body, 0)

    first = lax.broadcasted_iota(jnp.int32, (band, WCOLS), 1) < half
    for q in range(4):
        rho = (q % 2) * 2 + q // 2
        span = pl.ds(rho // 2 * WCOLS, WCOLS)
        hi, po = peak[:, span], power[:, span]
        if rho % 2 == 0:
            own[q] = jnp.where(first, hi, pltpu.roll(po, half, 1))
        else:
            own[q] = jnp.where(first, pltpu.roll(hi, half, 1), po)

    mine = pl.ds(pl.multiple_of(core * hb, hb), hb)
    theirs = pl.ds(pl.multiple_of((1 - core) * hb, hb), hb)
    def swap(k):
        q = lax.rem(me + k, bands)
        return pltpu.make_async_remote_copy(
            src_ref=own.at[q, theirs, :], dst_ref=sibling.at[q],
            send_sem=pair_send.at[k], recv_sem=pair_recv.at[k],
            device_id={"orient": 1 - core}, device_id_type=MESH,
        )

    for k in (2, 1, 3, 0):
        swap(k).start()
    first = lax.broadcasted_iota(jnp.int32, (hb, WCOLS), 1) < half

    def map_copy(k, source):
        dest = lax.rem(me + k, bands)
        return pltpu.make_async_remote_copy(
            src_ref=merged.at[dest], dst_ref=final.at[source, mine, :],
            send_sem=map_send.at[k], recv_sem=map_recv.at[source],
            device_id={"row": dest}, device_id_type=MESH,
        )

    def forward(source, rows):
        return pltpu.make_async_remote_copy(
            src_ref=final.at[source, rows, :], dst_ref=final.at[source, rows, :],
            send_sem=fwd_send.at[source], recv_sem=fwd_recv.at[source],
            device_id={"orient": 1 - core}, device_id_type=MESH,
        )

    for k in (2, 1, 3, 0):
        swap(k).wait_recv()
        q = lax.rem(me + k, bands)
        one, two = own[q, mine, :], sibling[q]
        total = jnp.where(first, jnp.maximum(one, two), one + two).astype(final.dtype)
        if k == 0:
            final[me, mine, :] = total
        else:
            merged[q] = total
            map_copy(k, me).start()
    forward(me, mine).start()
    for k in (1, 3, 2):
        source = lax.rem(me + k, bands)
        map_copy(k, source).wait_recv()
        forward(source, mine).start()
    for source in range(4):
        forward(source, theirs).wait_recv()
    for source in range(4):
        forward(source, mine).wait_send()
    for k in range(1, bands):
        map_copy(k, me).wait_send()
    for k in range(bands):
        swap(k).wait_send()

    def drain(o, carry):
        for k in range(1, bands):
            dest = lax.rem(me + k, bands)
            for h in range(PARTS):
                part_copy(k, dest, me, o, h).wait_send()
        return carry

    lax.fori_loop(0, share, drain, 0)


def assemble_kernel(maps, peak_ref, power_ref):
    half = WCOLS // 2
    first = lax.broadcasted_iota(jnp.int32, maps.shape[1:], 1) < half
    a, b = maps[0].astype(jnp.float32), maps[1].astype(jnp.float32)
    peak_ref[0, 0] = jnp.where(first, a, pltpu.roll(b, half, 1))
    power_ref[0, 0] = jnp.where(first, pltpu.roll(a, half, 1), b)


def shards_fused(spectra, bank, orient_index):
    band = spectra.shape[2]
    length = spectra.shape[3]
    tsize = bank.shape[1]
    bands = lax.axis_size("row")
    share = orient_index.shape[0] // lax.axis_size("orient")
    half = WCOLS // 2
    bf, f32 = jnp.bfloat16, jnp.float32

    small = np.arange(BLK)
    y = np.arange(tsize)
    kq = np.arange(length // 4)
    lane = np.arange(2 * WCOLS)
    lane_x = lane // WCOLS * half + lane % half
    is_im = lane % WCOLS >= half
    quarter = two_pi / 4
    steps = np.arange(length // BLK) * BLK
    short = np.arange(band // BLK) * BLK
    pb = band // PARTS
    at = np.arange(2 * band)
    col_j = at // (2 * pb) * pb + at % pb
    col_shift = np.where(at // pb % 2 == 0, 0.0, quarter)
    rho = np.repeat(np.arange(1, 4), WCOLS)
    spread = np.concatenate([np.arange(BLK) * 4 * BLK] + [4 * small + s for s in range(4)])
    w384 = np.concatenate(
        [
            factors(steps, y, length),
            factors(small, y, length),
            factors(short, rho, length),
            factors(small, rho, length),
        ],
        1,
    )
    w512 = factors(spread, kq, length)
    w256 = np.concatenate(
        [
            factors(steps, lane_x, length),
            factors(small, lane_x, length, np.where(is_im, -quarter, 0.0)),
            factors(small, lane_x, length, np.where(is_im, 0.0, quarter)),
        ],
        1,
    )
    w1024 = np.concatenate(
        [factors(short, col_j, band), factors(small, col_j, band, col_shift)], 1
    )
    tables = [w384, w512, w256, w1024]
    vmem = pl.BlockSpec(memory_space=pltpu.VMEM)
    hbm = pl.BlockSpec(memory_space=pl.ANY)
    dma = pltpu.SemaphoreType.DMA
    maps = pl.pallas_call(
        functools.partial(fused_kernel, (bands, share, band, length, tsize)),
        out_shape=jax.ShapeDtypeStruct((4, band, WCOLS), MAPS),
        in_specs=[pl.BlockSpec(memory_space=pltpu.SMEM)] + [hbm] * (2 + len(tables)),
        out_specs=vmem,
        scratch_shapes=[
            pltpu.VMEM(spectra.shape, bf),
            pltpu.VMEM(bank.shape, bf),
        ]
        + [pltpu.VMEM(table.shape, f32) for table in tables]
        + [
            pltpu.VMEM((2, band, tsize), bf),
            pltpu.VMEM((4, 2 * WCOLS, length // 4), bf),
            pltpu.VMEM((2, length, 2 * WCOLS), bf),
            pltpu.VMEM((band, 2 * band), bf),
            pltpu.VMEM((band, 2 * band), bf),
            pltpu.VMEM((band, 3 * WCOLS), f32),
            pltpu.VMEM((band, 3 * WCOLS), f32),
            pltpu.VMEM((tsize, 4 * WCOLS), bf),
            pltpu.VMEM((4, 2, band, 2 * WCOLS), bf),
            pltpu.VMEM((2, 2 * band // PARTS, length), bf),
            pltpu.VMEM((bands, share, band, WCOLS), bf),
            pltpu.VMEM((bands, share, band, WCOLS), bf),
            pltpu.VMEM((2 * band // PARTS, 2 * WCOLS), bf),
            pltpu.VMEM((2 * band // PARTS, 2 * WCOLS), bf),
            pltpu.VMEM((band, 2 * WCOLS), f32),
            pltpu.VMEM((band, 2 * WCOLS), f32),
            pltpu.VMEM((band, 2 * WCOLS), f32),
            pltpu.VMEM((4, band, WCOLS), f32),
            pltpu.VMEM((4, band // 2, WCOLS), f32),
            pltpu.VMEM((4, band // 2, WCOLS), MAPS),
            dma((6,)),
            dma((bands, share, PARTS)),
            dma((bands, share, PARTS)),
            dma((bands,)),
            dma((bands,)),
            dma((bands,)),
            dma((bands,)),
            dma((bands,)),
            dma((bands,)),
        ],
        compiler_params=pltpu.CompilerParams(
            collective_id=0, has_side_effects=True, vmem_limit_bytes=58 << 20
        ),
    )(orient_index, spectra, bank, *tables)
    out = jax.ShapeDtypeStruct((2, 1, band, WCOLS), f32)
    one_mic = pl.BlockSpec((1, 1, band, WCOLS), lambda m: (m, 0, 0, 0))
    return pl.pallas_call(
        assemble_kernel,
        grid=(2,),
        out_shape=(out, out),
        in_specs=[pl.BlockSpec((2, band, WCOLS), lambda m: (m, 0, 0))],
        out_specs=(one_mic, one_mic),
    )(maps)


def shards(spectra, bank, orient_index):
    fits = (
        lax.axis_size("row") == 4
        and lax.axis_size("orient") == 2
        and spectra.shape[0] == 2
        and spectra.shape[2] % 128 == 0
        and bank.shape[1] == 3 * WCOLS
        and spectra.shape[3] == 4 * spectra.shape[2]
    )
    body = shards_fused if fits else shards_general
    return body(spectra, bank, orient_index)


def solution(mesh):
    return jax.shard_map(
        shards,
        mesh=mesh,
        in_specs=(P(("grp", "mic"), None, "row", None), P(), P("grp")),
        out_specs=(P(("grp", "mic"), "row", None, None), P(("grp", "mic"), "row", None, None)),
        check_vma=False,
    )
```
